256 devices in a mesh: lon: 16 (over y_lo, z), lat: 16 (over x, y_hi, core).
Axes of the slice: x: 4, y: 4 (y_hi: 2, y_lo: 2; y = y_hi * 2 + y_lo), z: 8, core: 2. Of those that a mesh axis runs over, the one named last changes fastest.
Arguments:
- crosswise_speed_units: float32 [8, 256, 4096], P(None, 'lat', 'lon'), may hold values from -6 to 6
- poleward_speed_units: float32 [8, 256, 4096], P(None, 'lat', 'lon'), may hold values from -6 to 6
- thermal_anomaly: float32 [8, 256, 4096], P(None, 'lat', 'lon'), may hold values from -6 to 6
- saltiness_anomaly: float32 [8, 256, 4096], P(None, 'lat', 'lon'), may hold values from -6 to 6
- freeboard_elevation: float32 [256, 4096], P('lat', 'lon'), may hold values from -6 to 6
- barotropic_zonal_flow: float32 [256, 4096], P('lat', 'lon'), may hold values from -6 to 6
- barotropic_meridional_flow: float32 [256, 4096], P('lat', 'lon'), may hold values from -6 to 6
- submerged_layer_tally: int32 [256, 4096], P('lat', 'lon'), may hold values from 0 to 8
- seam_partner_index: int32 [4096], P('lon'), may hold values from 0 to 4095, as said below
Outputs:
- zonal_speed_final: float32 [8, 256, 4096], P(None, 'lat', 'lon')
- poleward_speed_final: float32 [8, 256, 4096], P(None, 'lat', 'lon')
- thermal_final: float32 [8, 256, 4096], P(None, 'lat', 'lon')
- saltiness_final: float32 [8, 256, 4096], P(None, 'lat', 'lon')
- freeboard_final: float32 [256, 4096], P('lat', 'lon')
- barotropic_zonal_final: float32 [256, 4096], P('lat', 'lon')
- barotropic_meridional_final: float32 [256, 4096], P('lat', 'lon')
The draws below stay inside these ranges and needn't reach their ends.
Inputs may be any that keep to these rules, and one draw needn't show every extreme that they name: seam_partner_index[seam_partner_index[c]] = c, and seam_partner_index[(c + 1) mod 4096] = (seam_partner_index[c] - 1) mod 4096 for every column c.
All inputs are finite; a program needn't handle non-finite values.
Results may differ from the reference program's by a relative error of at most 0.0003.
Values sent between devices are 32-bit elements; how exact they have to be, the bound alone decides.
A program may use at most 128 MiB of HBM per device.

```python
import jax
import jax.numpy as jnp
from jax import lax

VERTICAL_LAYERS = 8
SUBSTEPS = 12
MESH_YCOUNT = 256
MESH_XCOUNT = 4096


def draw_seam_partner_index(key, part):
    offset = jax.random.randint(jax.random.fold_in(key, 7), (), 0, MESH_XCOUNT)
    return jnp.remainder(offset - jnp.arange(MESH_XCOUNT, dtype=jnp.int32), MESH_XCOUNT).astype(jnp.int32)


def draw_submerged_layer_tally(key, part):
    selector = jax.random.randint(jax.random.fold_in(key, 11), (MESH_YCOUNT, MESH_XCOUNT), 0, 4)
    shallow = jax.random.randint(jax.random.fold_in(key, 12), (MESH_YCOUNT, MESH_XCOUNT), 0, VERTICAL_LAYERS + 1)
    return jnp.where(selector == 0, shallow, VERTICAL_LAYERS).astype(jnp.int32)


def shard_levels(key, dims, cuts, least, high):
    factor_of, own = 1.0, jax.random.fold_in(key, 6)
    for dim, parts in cuts:
        steps = jnp.exp(jax.random.uniform(jax.random.fold_in(own, dim), (parts,), jnp.float32, least / len(cuts), high / len(cuts)))
        factor_of = factor_of * jnp.repeat(steps, dims[dim] // parts).reshape([-1 if axis == dim else 1 for axis in range(len(dims))])
    return factor_of


def normal_values(own_key, shape, scale, bound, cuts=(), kind=jnp.bfloat16):
    gain = shard_levels(own_key, shape, cuts, -0.22, 0.18) if cuts else 1.0
    values = jax.random.normal(own_key, shape, jnp.float32) * scale * gain
    return jnp.minimum(jnp.maximum(values, -bound), bound).astype(kind)


def setup_inputs(seed: int = 0) -> dict:
    key_of = jax.random.split(jax.random.key(seed), 10)
    return {
        "crosswise_speed_units": normal_values(key_of[0], (VERTICAL_LAYERS, MESH_YCOUNT, MESH_XCOUNT), 1.0, 6.0, ((1, 16), (2, 16)), jnp.float32),
        "poleward_speed_units": normal_values(key_of[1], (VERTICAL_LAYERS, MESH_YCOUNT, MESH_XCOUNT), 1.0, 6.0, ((1, 16), (2, 16)), jnp.float32),
        "thermal_anomaly": normal_values(key_of[2], (VERTICAL_LAYERS, MESH_YCOUNT, MESH_XCOUNT), 1.0, 6.0, ((1, 16), (2, 16)), jnp.float32),
        "saltiness_anomaly": normal_values(key_of[3], (VERTICAL_LAYERS, MESH_YCOUNT, MESH_XCOUNT), 1.0, 6.0, ((1, 16), (2, 16)), jnp.float32),
        "freeboard_elevation": normal_values(key_of[4], (MESH_YCOUNT, MESH_XCOUNT), 1.0, 6.0, ((0, 16), (1, 16)), jnp.float32),
        "barotropic_zonal_flow": normal_values(key_of[5], (MESH_YCOUNT, MESH_XCOUNT), 1.0, 6.0, ((0, 16), (1, 16)), jnp.float32),
        "barotropic_meridional_flow": normal_values(key_of[6], (MESH_YCOUNT, MESH_XCOUNT), 1.0, 6.0, ((0, 16), (1, 16)), jnp.float32),
        "submerged_layer_tally": draw_submerged_layer_tally(jax.random.fold_in(key_of[9], 71), 0),
        "seam_partner_index": draw_seam_partner_index(jax.random.fold_in(key_of[9], 71), 0),
    }


COURANT = 0.15
PRESSURE_GAIN = 0.1
CORIOLIS = 0.3
WAVE_MASS = 1.2
WAVE_MOMENTUM = 1.2
EPSILON = 1e-6


def weno_face(far_up, near_up, centre, near_down, far_down):
    poly_zero = (2.0 * far_up - 7.0 * near_up + 11.0 * centre) / 6.0
    poly_one = (-near_up + 5.0 * centre + 2.0 * near_down) / 6.0
    poly_two = (2.0 * centre + 5.0 * near_down - far_down) / 6.0
    smooth_zero = 13.0 / 12.0 * (far_up - 2.0 * near_up + centre) ** 2 + 0.25 * (far_up - 4.0 * near_up + 3.0 * centre) ** 2
    smooth_one = 13.0 / 12.0 * (near_up - 2.0 * centre + near_down) ** 2 + 0.25 * (near_up - near_down) ** 2
    smooth_two = 13.0 / 12.0 * (centre - 2.0 * near_down + far_down) ** 2 + 0.25 * (3.0 * centre - 4.0 * near_down + far_down) ** 2
    weight_zero = 0.1 / (EPSILON + smooth_zero) ** 2
    weight_one = 0.6 / (EPSILON + smooth_one) ** 2
    weight_two = 0.3 / (EPSILON + smooth_two) ** 2
    return (weight_zero * poly_zero + weight_one * poly_one + weight_two * poly_two) / (weight_zero + weight_one + weight_two)


def face_fluxes(prognostic_bundle, velocity, wet_mask, along, length):
    def window(values, offset):
        return lax.slice_in_dim(values, offset, offset + length + 1, axis=along)

    face_speed = 0.5 * (window(velocity, 2) + window(velocity, 3)) * window(wet_mask, 2) * window(wet_mask, 3)
    upwind = weno_face(window(prognostic_bundle, 0), window(prognostic_bundle, 1), window(prognostic_bundle, 2), window(prognostic_bundle, 3), window(prognostic_bundle, 4))
    downwind = weno_face(window(prognostic_bundle, 5), window(prognostic_bundle, 4), window(prognostic_bundle, 3), window(prognostic_bundle, 2), window(prognostic_bundle, 1))
    fluxes = COURANT * face_speed * jnp.where(face_speed >= 0.0, upwind, downwind)
    return fluxes, face_speed


def wrap_columns(values, margin):
    return jnp.concatenate([values[..., -margin:], values, values[..., :margin]], axis=-1)


def fold_rows(values, margin, parity, seam_partner_index):
    southern = jnp.zeros(values.shape[:-2] + (margin, values.shape[-1]), jnp.float32)
    northern = parity * jnp.take(jnp.flip(values[..., -margin:, :], axis=-2), seam_partner_index, axis=-1)
    return jnp.concatenate([southern, values, northern], axis=-2)


def reference(crosswise_speed_units, poleward_speed_units, thermal_anomaly, saltiness_anomaly, freeboard_elevation, barotropic_zonal_flow, barotropic_meridional_flow, submerged_layer_tally, seam_partner_index):
    levels, lat_count, lon_count = crosswise_speed_units.shape
    level_index = lax.broadcasted_iota(jnp.int32, (levels, 1, 1), 0)
    submerged_indicator = (level_index < submerged_layer_tally[None]).astype(jnp.float32)
    wet_column = (submerged_layer_tally > 0).astype(jnp.float32)
    row_index = lax.broadcasted_iota(jnp.int32, (lat_count, 1), 0).astype(jnp.float32)
    coriolis = CORIOLIS * (2.0 * (row_index + 0.5) / lat_count - 1.0)
    field_parity = jnp.array([-1.0, -1.0, 1.0, 1.0], jnp.float32)[:, None, None]
    seawater_buoyancy_mass = 0.8 * saltiness_anomaly - 0.2 * thermal_anomaly
    pressure = jnp.cumsum(seawater_buoyancy_mass, axis=0) - 0.5 * seawater_buoyancy_mass
    prognostic_bundle = jnp.stack([crosswise_speed_units, poleward_speed_units, thermal_anomaly, saltiness_anomaly], axis=1)

    def horizontal(inputs):
        level_fields, wet_mask, pressure_level = inputs
        east_west = wrap_columns(level_fields, 3)
        wet_east = wrap_columns(wet_mask, 3)
        flux_east, speed_east = face_fluxes(east_west, east_west[0:1], wet_east[None], 2, lon_count)
        north_south = fold_rows(level_fields, 3, field_parity, seam_partner_index)
        wet_north = fold_rows(wet_mask, 3, 1.0, seam_partner_index)
        flux_north, speed_north = face_fluxes(north_south, north_south[1:2], wet_north[None], 1, lat_count)
        prognostic_rate = -(flux_east[:, :, 1:] - flux_east[:, :, :-1]) - (flux_north[:, 1:, :] - flux_north[:, :-1, :])
        spread = (speed_east[0, :, 1:] - speed_east[0, :, :-1]) + (speed_north[0, 1:, :] - speed_north[0, :-1, :])
        press_east = wrap_columns(pressure_level, 1)
        press_north = fold_rows(pressure_level, 1, 1.0, seam_partner_index)
        grad_east = 0.5 * (press_east[:, 2:] - press_east[:, :-2])
        grad_north = 0.5 * (press_north[2:, :] - press_north[:-2, :])
        return prognostic_rate, spread, grad_east, grad_north

    prognostic_rate, spread, grad_east, grad_north = lax.map(horizontal, (prognostic_bundle, submerged_indicator, pressure))
    upward = -jnp.flip(jnp.cumsum(jnp.flip(spread, 0), axis=0), 0)
    interior = COURANT * upward[1:, None] * 0.5 * (prognostic_bundle[:-1] + prognostic_bundle[1:])
    boundary = jnp.zeros((1,) + interior.shape[1:], jnp.float32)
    vertical_flux = jnp.concatenate([boundary, interior, boundary], axis=0)
    prognostic_rate = prognostic_rate - (vertical_flux[:-1] - vertical_flux[1:])

    force_zonal = prognostic_rate[:, 0] + coriolis * poleward_speed_units - PRESSURE_GAIN * grad_east
    force_merid = prognostic_rate[:, 1] - coriolis * crosswise_speed_units - PRESSURE_GAIN * grad_north
    column = jnp.maximum(submerged_layer_tally, 1).astype(jnp.float32)
    mean_zonal = jnp.sum(submerged_indicator * force_zonal, axis=0) / column
    mean_merid = jnp.sum(submerged_indicator * force_merid, axis=0) / column
    thickness = submerged_layer_tally.astype(jnp.float32) / levels

    def substep(wave_state, unused):
        sea_level, zonal_flow, merid_flow = wave_state
        mass_east = wrap_columns(thickness * zonal_flow, 1)
        mass_north = fold_rows(thickness * merid_flow, 1, -1.0, seam_partner_index)
        spread_wave = 0.5 * (mass_east[:, 2:] - mass_east[:, :-2]) + 0.5 * (mass_north[2:, :] - mass_north[:-2, :])
        next_level = wet_column * (sea_level - WAVE_MASS * spread_wave)
        level_east = wrap_columns(next_level, 1)
        level_north = fold_rows(next_level, 1, 1.0, seam_partner_index)
        next_zonal = wet_column * (zonal_flow - WAVE_MOMENTUM * 0.5 * (level_east[:, 2:] - level_east[:, :-2]) + (coriolis * merid_flow + mean_zonal) / SUBSTEPS)
        next_merid = wet_column * (merid_flow - WAVE_MOMENTUM * 0.5 * (level_north[2:, :] - level_north[:-2, :]) + (-coriolis * zonal_flow + mean_merid) / SUBSTEPS)
        return (next_level, next_zonal, next_merid), None

    final_state, unused = lax.scan(substep, (freeboard_elevation, barotropic_zonal_flow, barotropic_meridional_flow), None, length=SUBSTEPS)
    freeboard_final, barotropic_zonal_final, barotropic_meridional_final = final_state
    zonal_speed_final = submerged_indicator * (crosswise_speed_units + force_zonal - mean_zonal + (barotropic_zonal_final - barotropic_zonal_flow))
    poleward_speed_final = submerged_indicator * (poleward_speed_units + force_merid - mean_merid + (barotropic_meridional_final - barotropic_meridional_flow))
    thermal_final = submerged_indicator * (thermal_anomaly + prognostic_rate[:, 2])
    saltiness_final = submerged_indicator * (saltiness_anomaly + prognostic_rate[:, 3])
    return (zonal_speed_final, poleward_speed_final, thermal_final, saltiness_final, freeboard_final, barotropic_zonal_final, barotropic_meridional_final)
```

```python
import functools

import jax
import jax.numpy as jnp
from jax import lax
from jax.experimental import pallas as pl
from jax.experimental.pallas import tpu as pltpu
from jax.sharding import PartitionSpec as P

MESH = pl.DeviceIdType.MESH

SUBSTEPS = 12
COURANT = 0.15
PRESSURE_GAIN = 0.1
CORIOLIS = 0.3
WAVE_MASS = 1.2
WAVE_MOMENTUM = 1.2
EPSILON = 1e-06

LEVELS, ROWS, COLS = 8, 16, 256
MARGIN = 2 * SUBSTEPS
WIDE = ROWS + 2 * MARGIN
LANES = 128

SEA, ZON, MER, TALLY, MEANZ, MEANM = range(6)


def weno_flux(em2, em1, e0, ep1, ep2, q0, q1, carry, drift, ahead):
    far = jnp.where(ahead, em2, ep2)
    near = jnp.where(ahead, em1, ep1)
    down = jnp.where(ahead, ep1, em1)
    centre = jnp.where(ahead, q0, q1)
    b0 = far * (4.0 * far - 11.0 * near) + (10.0 * near * near + 3.0 * EPSILON)
    b1 = near * (4.0 * near - 5.0 * e0) + (4.0 * e0 * e0 + 3.0 * EPSILON)
    b2 = e0 * (10.0 * e0 - 11.0 * down) + (4.0 * down * down + 3.0 * EPSILON)
    m0 = b1 * b2
    m1 = b0 * b2
    m2 = b0 * b1
    s0 = m0 * m0
    s1 = 6.0 * (m1 * m1)
    s2 = 3.0 * (m2 * m2)
    top = s0 * (5.0 * near - 2.0 * far) + s1 * (near + 2.0 * e0) + s2 * (4.0 * e0 - down)
    return carry * centre + drift * (top / (s0 + s1 + s2))


def kernel(
    lon_size,
    lat_size,
    turn,
    seam_ref,
    u_in,
    v_in,
    t_in,
    s_in,
    sea_in,
    zon_in,
    mer_in,
    tally_in,
    u_out,
    v_out,
    t_out,
    s_out,
    sea_out,
    zon_out,
    mer_out,
    raw,
    tally_raw,
    cells,
    edge_send,
    edge_recv,
    halo,
    face_west,
    flux_north,
    part,
    rim,
    fold_cells,
    fold_rim,
    wave,
    done,
    flat,
    in_sem,
    out_sem,
    edge_sem,
    band_sem,
    rim_sem,
    fold_sem,
    fold_rim_sem,
    fold_tall_sem,
):
    lon = lax.axis_index("lon")
    lat = lax.axis_index("lat")
    top = lat == lat_size - 1
    below = lat == lat_size - 2
    f32 = jnp.float32

    loads = []
    for f, ref in enumerate((u_in, v_in, t_in, s_in)):
        for t in range(2):
            loads.append(
                pltpu.make_async_copy(
                    ref.at[:, t * LANES : (t + 1) * LANES], raw.at[f, t], in_sem.at[2 * f + t]
                )
            )
    for f, ref in enumerate((sea_in, zon_in, mer_in)):
        loads.append(
            pltpu.make_async_copy(
                ref, rim.at[f, MARGIN : MARGIN + ROWS, 0:COLS], in_sem.at[8 + f]
            )
        )
    loads.append(pltpu.make_async_copy(tally_in, tally_raw, in_sem.at[11]))
    for copy in loads:
        copy.start()

    shifts = [(a, b) for a in (1, -1, 2, -2, 0) for b in (0, 1, -1) if (a, b) != (0, 0)]

    def lat_ok(a):
        return jnp.logical_and(lat + a >= 0, lat + a <= lat_size - 1)

    def when(cond, body):
        if cond is True:
            body()
        else:
            pl.when(cond)(body)

    def peer(a, b):
        return {"lat": lat + a, "lon": lax.rem(lon + b + lon_size, lon_size)}

    fold_slots = list(range(4))

    def fold_peer(s):
        return lax.rem(turn - lon + s - 2 + 2 * lon_size, lon_size)

    barrier = pltpu.get_barrier_semaphore()

    def greet(lat_to, lon_to):
        pl.semaphore_signal(
            barrier, inc=1, device_id={"lat": lat_to, "lon": lon_to}, device_id_type=MESH
        )

    for a, b in shifts:

        def hello(a=a, b=b):
            to = peer(a, b)
            greet(to["lat"], to["lon"])

        when(True if a == 0 else lat_ok(a), hello)

    @pl.when(top)
    def _():
        for s in fold_slots:
            q = fold_peer(s)

            @pl.when(q != lon)
            def _():
                greet(lat, q)

            greet(lat - 1, q)

    @pl.when(below)
    def _():
        for s in fold_slots:
            greet(lat + 1, fold_peer(s))

    @pl.when(lat == 0)
    def _():
        cells[:, 0:3] = jnp.zeros((5, 3, 2, LEVELS, LANES), f32)
        rim[:, 0:MARGIN, :] = jnp.zeros((6, MARGIN, 512), f32)

    @pl.when(lat == 1)
    def _():
        rim[:, 0:8, :] = jnp.zeros((6, 8, 512), f32)

    level = lax.broadcasted_iota(jnp.int32, (LEVELS, LANES), 0)
    lane = lax.broadcasted_iota(jnp.int32, (LEVELS, LANES), 1)

    for copy in loads:
        copy.wait()
    for t in range(2):
        tally = tally_raw[:, t * LANES : (t + 1) * LANES].astype(f32)
        rim[TALLY, MARGIN : MARGIN + ROWS, t * LANES : (t + 1) * LANES] = tally
        flat[2, t] = tally
    level_real = level.astype(f32)

    def arrange(r, _):
        for t in range(2):
            for f in range(4):
                cells[f, r + 3, t] = raw[f, t, pl.ds(r, LEVELS, stride=ROWS), :]
            tally_row = flat[2, t, pl.ds(r, 1), :]
            cells[4, r + 3, t] = jnp.where(level_real < tally_row, 1.0, 0.0)
        return _

    lax.fori_loop(0, ROWS, arrange, 0)

    triple = lax.shift_right_logical(lane * 43, 7)
    for f in range(5):
        left = jnp.zeros((LEVELS, LANES), f32)
        right = jnp.zeros((LEVELS, LANES), f32)
        for r in range(ROWS):
            mine = triple == r
            west_tile = cells[f, r + 3, 0]
            east_tile = cells[f, r + 3, 1]
            if r:
                west_tile = pltpu.roll(west_tile, 3 * r, 1)
            left = jnp.where(mine, west_tile, left)
            right = jnp.where(mine, pltpu.roll(east_tile, 3 * r + 3, 1), right)
        edge_send[0, f] = left
        edge_send[1, f] = right

    count = jnp.int32(0)
    for a, b in shifts:
        count = count + (1 if a == 0 else lat_ok(a).astype(jnp.int32))
    fold_count = jnp.int32(0)
    for s in fold_slots:
        fold_count = fold_count + (fold_peer(s) != lon).astype(jnp.int32) + 1
    count = count + jnp.where(top, fold_count, 0)
    count = count + jnp.where(below, len(fold_slots), 0)
    pl.semaphore_wait(barrier, count)

    def edge_copy(side):
        return pltpu.make_async_remote_copy(
            src_ref=edge_send.at[side],
            dst_ref=edge_recv.at[side],
            send_sem=edge_sem.at[0, side],
            recv_sem=edge_sem.at[1, side],
            device_id=peer(0, -1 if side == 0 else 1),
            device_id_type=MESH,
        )

    def band_copy(side):
        src, dst = ((ROWS, ROWS + 3), (0, 3)) if side == 0 else ((3, 6), (ROWS + 3, ROWS + 6))
        return pltpu.make_async_remote_copy(
            src_ref=cells.at[:, src[0] : src[1]],
            dst_ref=cells.at[:, dst[0] : dst[1]],
            send_sem=band_sem.at[0, side],
            recv_sem=band_sem.at[1, side],
            device_id=peer(1 if side == 0 else -1, 0),
            device_id_type=MESH,
        )

    def rim_copy(phase, n):
        a, b = shifts[n]
        first, last = (SEA, MEANZ) if phase == 0 else (MEANZ, MEANM + 1)
        src_rows, dst_rows = {
            1: ((MARGIN, MARGIN + 16), (8, 24)),
            2: ((MARGIN + 8, MARGIN + 16), (0, 8)),
            0: ((MARGIN, MARGIN + 16), (MARGIN, MARGIN + 16)),
            -1: ((MARGIN, MARGIN + 16), (MARGIN + 16, MARGIN + 32)),
            -2: ((MARGIN, MARGIN + 8), (MARGIN + 32, MARGIN + 40)),
        }[a]
        src_cols, dst_cols = {
            0: ((0, 256), (0, 256)),
            1: ((128, 256), (384, 512)),
            -1: ((0, 128), (256, 384)),
        }[b]
        return pltpu.make_async_remote_copy(
            src_ref=rim.at[first:last, src_rows[0] : src_rows[1], src_cols[0] : src_cols[1]],
            dst_ref=rim.at[first:last, dst_rows[0] : dst_rows[1], dst_cols[0] : dst_cols[1]],
            send_sem=rim_sem.at[phase, 0, n],
            recv_sem=rim_sem.at[phase, 1, n],
            device_id=peer(a, b),
            device_id_type=MESH,
        )

    cell_slots = [1, 2]

    def pair(src, dst, send_sem, recv_sem, s, lat_to, same_lat):
        q = fold_peer(s)

        def remote():
            return pltpu.make_async_remote_copy(
                src_ref=src,
                dst_ref=dst,
                send_sem=send_sem,
                recv_sem=recv_sem,
                device_id={"lat": lat_to, "lon": q},
                device_id_type=MESH,
            )

        local = (lambda: pltpu.make_async_copy(src, dst, recv_sem)) if same_lat else None
        return remote, local, q == lon

    def start_pair(p):
        remote, local, own = p
        if local is None:
            remote().start()
        else:

            @pl.when(jnp.logical_not(own))
            def _():
                remote().start()

            @pl.when(own)
            def _():
                local().start()

    def sent_pair(p):
        remote, local, own = p
        if local is None:
            remote().wait_send()
        else:

            @pl.when(jnp.logical_not(own))
            def _():
                remote().wait_send()

    def fold_cell_pair(s):
        return pair(
            cells.at[:, ROWS : ROWS + 3],
            fold_cells.at[s],
            fold_sem.at[0, s],
            fold_sem.at[1, s],
            s,
            lat,
            True,
        )

    def fold_rim_pair(phase, kind, s):
        first, last = (SEA, MEANZ) if phase == 0 else (MEANZ, MEANM + 1)
        rows = (MARGIN, MARGIN + 16) if kind == 0 else (MARGIN + 8, MARGIN + 16)
        dst_rows = {0: (0, 16), 1: (8, 16), 2: (16, 24)}[kind]
        sems = fold_tall_sem if kind == 0 else fold_rim_sem
        return pair(
            rim.at[first:last, rows[0] : rows[1], 0:COLS],
            fold_rim.at[s, first:last, dst_rows[0] : dst_rows[1]],
            sems.at[phase, 0, 0, s],
            sems.at[phase, 0, 1, s],
            s,
            lat + {0: 0, 1: -1, 2: 1}[kind],
            kind == 0,
        )

    def rim_start(phase):
        for n, (a, b) in enumerate(shifts):
            when(True if a == 0 else lat_ok(a), lambda n=n: rim_copy(phase, n).start())

    def rim_fold_start(phase):
        @pl.when(top)
        def _():
            for s in fold_slots:
                start_pair(fold_rim_pair(phase, 0, s))
                start_pair(fold_rim_pair(phase, 1, s))

        @pl.when(below)
        def _():
            for s in fold_slots:
                start_pair(fold_rim_pair(phase, 2, s))

    def rim_arrived(phase):
        for n, (a, b) in enumerate(shifts):
            when(True if a == 0 else lat_ok(-a), lambda n=n: rim_copy(phase, n).wait_recv())

    def rim_fold_arrived(phase):
        @pl.when(top)
        def _():
            for s in fold_slots:
                fold_rim_pair(phase, 0, s)[0]().wait_recv()
                fold_rim_pair(phase, 2, s)[0]().wait_recv()

        @pl.when(below)
        def _():
            for s in fold_slots:
                fold_rim_pair(phase, 1, s)[0]().wait_recv()

    def rim_sent(phase):
        for n, (a, b) in enumerate(shifts):
            when(True if a == 0 else lat_ok(a), lambda n=n: rim_copy(phase, n).wait_send())

        @pl.when(top)
        def _():
            for s in fold_slots:
                sent_pair(fold_rim_pair(phase, 0, s))
                sent_pair(fold_rim_pair(phase, 1, s))

        @pl.when(below)
        def _():
            for s in fold_slots:
                sent_pair(fold_rim_pair(phase, 2, s))

    for side in range(2):
        edge_copy(side).start()

    @pl.when(top)
    def _():
        for s in cell_slots:
            start_pair(fold_cell_pair(s))

    when(lat_ok(1), lambda: band_copy(0).start())
    when(lat_ok(-1), lambda: band_copy(1).start())
    rim_start(0)
    rim_fold_start(0)

    first_partner = jnp.full((LEVELS, LANES), seam_ref[0], jnp.int32)
    upper = jnp.bitwise_and(first_partner, LANES) != 0
    base_lanes = jnp.bitwise_and(first_partner, LANES - 1)
    same_tile = lane <= base_lanes
    steps = [jnp.bitwise_and(base_lanes + 1, 1 << n) != 0 for n in range(7)]
    mirror = LANES - 1 - lane

    def turn_lanes(low, high):
        x = jnp.take_along_axis(jnp.where(upper, high, low), mirror, axis=1)
        for n in range(7):
            x = jnp.where(steps[n], pltpu.roll(x, 1 << n, 1), x)
        return x

    row_bit1 = jnp.bitwise_and(level, 1) == 0
    row_bit2 = jnp.bitwise_and(level, 2) == 0

    def flip_rows(x):
        x = pltpu.roll(x, 4, 0)
        x = jnp.where(row_bit2, pltpu.roll(x, 6, 0), pltpu.roll(x, 2, 0))
        return jnp.where(row_bit1, pltpu.roll(x, 7, 0), pltpu.roll(x, 1, 0))

    def north_face(face):
        speeds = []
        for t in range(2):
            speed = (
                0.5
                * (cells[1, face + 2, t] + cells[1, face + 3, t])
                * cells[4, face + 2, t]
                * cells[4, face + 3, t]
            )
            flux_north[4, face, t] = speed
            speeds.append(
                (COURANT * speed, (COURANT / 6.0) * jnp.abs(speed), speed >= 0.0)
            )
        for f in range(4):
            for t in range(2):
                q = [cells[f, face + n, t] for n in range(6)]
                e = [q[n + 1] - q[n] for n in range(5)]
                flux_north[f, face, t] = weno_flux(*e, q[2], q[3], *speeds[t])

    def north_loop(face, _):
        north_face(face)
        return _

    lax.fori_loop(3, 14, north_loop, 0)

    for side in range(2):
        edge_copy(side).wait_recv()

    def back(x, n):
        return pltpu.roll(x, LANES - n, 1)

    packed = []
    for f in range(5):
        west = edge_recv[1, f]
        own = edge_send[0, f]
        packed.append((west, own))
    speed = 0.5 * (back(packed[0][0], 2) + packed[0][1]) * back(packed[4][0], 2) * packed[4][1]
    face_west[4] = speed
    for f in range(4):
        west, own = packed[f]
        inner = back(west, 2)
        ew = back(west, 1) - west
        eo = back(own, 1) - own
        face_west[f] = weno_flux(
            ew,
            back(ew, 1),
            own - inner,
            eo,
            back(eo, 1),
            inner,
            own,
            COURANT * speed,
            (COURANT / 6.0) * jnp.abs(speed),
            speed >= 0.0,
        )

    first_lane = lane == 0
    last_lane = lane == LANES - 1

    def unpack(r, _):
        for f in range(5):
            east = pltpu.roll(edge_recv[0, f], LANES - 3 * r, 1)
            west = pltpu.roll(edge_recv[1, f], LANES - 3 - 3 * r, 1)
            halo[f, r] = jnp.where(lane < LANES // 2, east, west)
        return _

    lax.fori_loop(0, ROWS, unpack, 0)

    def ahead_1(x):
        turned = [pltpu.roll(v, LANES - 1, 1) for v in x]
        return [jnp.where(last_lane, turned[(n + 1) % 3], turned[n]) for n in range(3)]

    def ahead_2(x):
        turned = [pltpu.roll(v, LANES - 2, 1) for v in x]
        return [
            jnp.where(lane >= LANES - 2, turned[(n + 1) % 3], turned[n]) for n in range(2)
        ]

    def behind_1(x):
        turned = [pltpu.roll(v, 1, 1) for v in x]
        return [jnp.where(first_lane, turned[(n + 2) % 3], turned[n]) for n in range(2)]

    def behind_2(x):
        turned = [pltpu.roll(v, 2, 1) for v in x]
        return [jnp.where(lane < 2, turned[(n + 2) % 3], turned[n]) for n in range(2)]

    def east_loop(r, _):
        wet = [cells[4, r + 3, 0], cells[4, r + 3, 1], halo[4, r]]
        wet_next = ahead_1(wet)
        gaps, nexts, firsts = [], [], []
        for f in range(4):
            q = [cells[f, r + 3, 0], cells[f, r + 3, 1], halo[f, r]]
            nxt = ahead_1(q)
            firsts.append(q)
            nexts.append(nxt)
            gaps.append([nxt[n] - q[n] for n in range(3)])
        speeds = []
        for t in range(2):
            speed = 0.5 * (firsts[0][t] + nexts[0][t]) * wet[t] * wet_next[t]
            speeds.append(speed)
        behind = []

        def difference(x, first):
            turned = [pltpu.roll(v, 1, 1) for v in x]
            return (
                x[0] - jnp.where(first_lane, first, turned[0]),
                x[1] - jnp.where(first_lane, turned[0], turned[1]),
            )

        def west_of(f):
            return pltpu.roll(face_west[f], LANES - 3 * r, 1)

        spread = difference(speeds, west_of(4))
        for t in range(2):
            part[4, r, t] = spread[t]
        for f in range(4):
            e = gaps[f]
            em1 = behind_1(e)
            em2 = behind_2(e)
            ep1 = ahead_1(e)
            ep2 = ahead_2(e)
            behind.append(em1)
            flux = [
                weno_flux(
                    em2[t],
                    em1[t],
                    e[t],
                    ep1[t],
                    ep2[t],
                    firsts[f][t],
                    nexts[f][t],
                    COURANT * speeds[t],
                    (COURANT / 6.0) * jnp.abs(speeds[t]),
                    speeds[t] >= 0.0,
                )
                for t in range(2)
            ]
            lost = difference(flux, west_of(f))
            for t in range(2):
                part[f, r, t] = lost[t]
        for t in range(2):
            part[5, r, t] = 0.8 * (gaps[3][t] + behind[3][t]) - 0.2 * (
                gaps[2][t] + behind[2][t]
            )
        return _

    lax.fori_loop(0, ROWS, east_loop, 0)

    when(lat_ok(-1), lambda: band_copy(0).wait_recv())
    when(lat_ok(1), lambda: band_copy(1).wait_recv())

    @pl.when(top)
    def _():
        for s in cell_slots:
            fold_cell_pair(s)[0]().wait_recv()
        for f in range(5):
            for g in range(3):

                def tile(n):
                    return fold_cells[n // 2, f, 2 - g, n % 2]

                turned = [turn_lanes(tile(4 - n), tile(5 - n)) for n in range(3)]
                for t in range(2):
                    value = jnp.where(same_tile, turned[t], turned[t + 1])
                    cells[f, ROWS + 3 + g, t] = -value if f < 2 else value

    def outer_loop(n, _):
        north_face(n)
        north_face(n + 14)
        return _

    lax.fori_loop(0, 3, outer_loop, 0)

    def down_sum(x):
        for s in (1, 2, 4):
            x = x + jnp.where(level >= s, pltpu.roll(x, s, 0), 0.0)
        return x

    def up_sum(x):
        for s in (1, 2, 4):
            x = x + jnp.where(level < LEVELS - s, pltpu.roll(x, LEVELS - s, 0), 0.0)
        return x

    total_rows = ROWS * lat_size

    def combine(r, _):
        row = (lat * ROWS + r).astype(f32)
        coriolis = CORIOLIS * (2.0 * (row + 0.5) / total_rows - 1.0)
        for t in range(2):
            q = [cells[f, r + 3, t] for f in range(4)]
            wet = cells[4, r + 3, t]
            spread = part[4, r, t] + (flux_north[4, r + 1, t] - flux_north[4, r, t])
            lift = jnp.where(level >= 1, (-0.5 * COURANT) * up_sum(spread), 0.0)
            rates = []
            for f in range(4):
                vertical = lift * (pltpu.roll(q[f], 1, 0) + q[f])
                rates.append(
                    (pltpu.roll(vertical, LEVELS - 1, 0) - vertical)
                    - part[f, r, t]
                    - (flux_north[f, r + 1, t] - flux_north[f, r, t])
                )
            slope_east = part[5, r, t]
            slope_north = 0.8 * (cells[3, r + 4, t] - cells[3, r + 2, t]) - 0.2 * (
                cells[2, r + 4, t] - cells[2, r + 2, t]
            )
            grad_east = 0.5 * (down_sum(slope_east) - 0.5 * slope_east)
            grad_north = 0.5 * (down_sum(slope_north) - 0.5 * slope_north)
            force_zonal = rates[0] + coriolis * q[1] - PRESSURE_GAIN * grad_east
            force_merid = rates[1] - coriolis * q[0] - PRESSURE_GAIN * grad_north
            flat[0, t, pl.ds(r, 1), :] = jnp.sum(wet * force_zonal, axis=0, keepdims=True)
            flat[1, t, pl.ds(r, 1), :] = jnp.sum(wet * force_merid, axis=0, keepdims=True)
            part[0, r, t] = q[0] + force_zonal
            part[1, r, t] = q[1] + force_merid
            done[2, t, pl.ds(r, LEVELS, stride=ROWS), :] = wet * (q[2] + rates[2])
            done[3, t, pl.ds(r, LEVELS, stride=ROWS), :] = wet * (q[3] + rates[3])
        return _

    lax.fori_loop(0, ROWS, combine, 0)

    own_rows = slice(MARGIN, MARGIN + ROWS)
    for t in range(2):
        column = jnp.maximum(flat[2, t], 1.0)
        for f in range(2):
            rim[MEANZ + f, own_rows, t * LANES : (t + 1) * LANES] = flat[f, t] / column

    rim_fold_start(1)
    rim_start(1)

    stores = []
    for f, ref in ((2, t_out), (3, s_out)):
        for t in range(2):
            stores.append(
                pltpu.make_async_copy(
                    done.at[f, t], ref.at[:, t * LANES : (t + 1) * LANES], out_sem.at[2 * f + t]
                )
            )
    for copy in stores:
        copy.start()

    def unfold(fields, ghost_tiles):
        for f in fields:
            sign = -1.0 if f in (ZON, MER, MEANZ, MEANM) else 1.0
            for to, source in ghost_tiles:

                def tile(n):
                    at = slice((n % 2) * LANES, (n % 2 + 1) * LANES)
                    return fold_rim[n // 2, f, source : source + 8, at]

                turned = {n: flip_rows(turn_lanes(tile(n + 4), tile(n + 5))) for n in range(-3, 2)}
                for near, at in ((0, 0), (-1, 1), (-2, 2), (1, 3)):
                    value = jnp.where(same_tile, turned[near], turned[near - 1]) * sign
                    rim[f, to : to + 8, at * LANES : (at + 1) * LANES] = value

    top_tiles = ((40, 8), (48, 0), (56, 16))
    below_tiles = ((56, 8),)

    rim_arrived(0)
    rim_fold_arrived(0)

    @pl.when(top)
    def _():
        unfold((SEA, ZON, MER, TALLY), top_tiles)

    @pl.when(below)
    def _():
        unfold((SEA, ZON, MER, TALLY), below_tiles)

    half = lax.broadcasted_iota(jnp.int32, (WIDE, LANES), 1) < LANES // 2

    def widened(f):
        side = jnp.where(half, rim[f, :, 256:384], rim[f, :, 384:512])
        return jnp.concatenate([rim[f, :, 0:COLS], side], axis=1)

    for f in (SEA, ZON, MER):
        wave[f] = widened(f)

    rim_arrived(1)
    rim_fold_arrived(1)

    @pl.when(top)
    def _():
        unfold((MEANZ, MEANM), top_tiles)

    @pl.when(below)
    def _():
        unfold((MEANZ, MEANM), below_tiles)

    width = COLS + LANES
    wide_tally = widened(TALLY)
    rows = lax.broadcasted_iota(jnp.int32, (WIDE, width), 0) + (lat * ROWS - MARGIN)
    rows = jnp.minimum(rows, 2 * total_rows - 1 - rows).astype(f32)
    wave[3] = wide_tally * (0.5 * WAVE_MASS / LEVELS)
    wave[4] = jnp.where(wide_tally > 0.0, 1.0, 0.0)
    wave[5] = (CORIOLIS / SUBSTEPS) * (2.0 * (rows + 0.5) / total_rows - 1.0)
    wave[6] = widened(MEANZ) * (1.0 / SUBSTEPS)
    wave[7] = widened(MEANM) * (1.0 / SUBSTEPS)

    def east_difference(x):
        return pltpu.roll(x, width - 1, 1) - pltpu.roll(x, 1, 1)

    def north_difference(x):
        return pltpu.roll(x, WIDE - 1, 0) - pltpu.roll(x, 1, 0)

    def substep(n, _):
        thick = wave[3]
        wet = wave[4]
        zonal = wave[ZON]
        merid = wave[MER]
        level_next = wet * (
            wave[SEA] - (east_difference(thick * zonal) + north_difference(thick * merid))
        )
        turn_rate = wave[5]
        wave[SEA] = level_next
        wave[ZON] = wet * (
            zonal
            - (0.5 * WAVE_MOMENTUM) * east_difference(level_next)
            + (turn_rate * merid + wave[6])
        )
        wave[MER] = wet * (
            merid
            - (0.5 * WAVE_MOMENTUM) * north_difference(level_next)
            + (wave[7] - turn_rate * zonal)
        )
        return _

    lax.fori_loop(0, SUBSTEPS, substep, 0)

    for f, ref in enumerate((sea_out, zon_out, mer_out)):
        copy = pltpu.make_async_copy(
            wave.at[f, own_rows, 0:COLS], ref, out_sem.at[8 + f]
        )
        copy.start()
        stores.append(copy)
    for f in range(2):
        for t in range(2):
            lanes = slice(t * LANES, (t + 1) * LANES)
            flat[f, t] = (
                wave[ZON + f, own_rows, lanes]
                - rim[ZON + f, own_rows, lanes]
                - rim[MEANZ + f, own_rows, lanes]
            )

    def finish(r, _):
        for t in range(2):
            wet = cells[4, r + 3, t]
            for f in range(2):
                shift = flat[f, t, pl.ds(r, 1), :]
                done[f, t, pl.ds(r, LEVELS, stride=ROWS), :] = wet * (part[f, r, t] + shift)
        return _

    lax.fori_loop(0, ROWS, finish, 0)

    for f, ref in ((0, u_out), (1, v_out)):
        for t in range(2):
            copy = pltpu.make_async_copy(
                done.at[f, t], ref.at[:, t * LANES : (t + 1) * LANES], out_sem.at[2 * f + t]
            )
            copy.start()
            stores.append(copy)

    for side in range(2):
        edge_copy(side).wait_send()
    when(lat_ok(1), lambda: band_copy(0).wait_send())
    when(lat_ok(-1), lambda: band_copy(1).wait_send())

    @pl.when(top)
    def _():
        for s in cell_slots:
            sent_pair(fold_cell_pair(s))

    rim_sent(0)
    rim_sent(1)
    for copy in stores:
        copy.wait()


def step_call(lon_size, lat_size, turn, collective_id):
    slots = 4
    f32 = jnp.float32
    deep = jax.ShapeDtypeStruct((LEVELS * ROWS, COLS), f32)
    flat = jax.ShapeDtypeStruct((ROWS, COLS), f32)
    anywhere = pl.BlockSpec(memory_space=pl.ANY)
    dma = pltpu.SemaphoreType.DMA
    return pl.pallas_call(
        functools.partial(kernel, lon_size, lat_size, turn),
        out_shape=(deep,) * 4 + (flat,) * 3,
        in_specs=[pl.BlockSpec(memory_space=pltpu.SMEM)] + [anywhere] * 8,
        out_specs=(anywhere,) * 7,
        scratch_shapes=[
            pltpu.VMEM((4, 2, LEVELS * ROWS, LANES), f32),
            pltpu.VMEM((ROWS, COLS), jnp.int32),
            pltpu.VMEM((5, ROWS + 6, 2, LEVELS, LANES), f32),
            pltpu.VMEM((2, 5, LEVELS, LANES), f32),
            pltpu.VMEM((2, 5, LEVELS, LANES), f32),
            pltpu.VMEM((5, ROWS, LEVELS, LANES), f32),
            pltpu.VMEM((5, LEVELS, LANES), f32),
            pltpu.VMEM((5, ROWS + 1, 2, LEVELS, LANES), f32),
            pltpu.VMEM((6, ROWS, 2, LEVELS, LANES), f32),
            pltpu.VMEM((6, WIDE, 2 * COLS), f32),
            pltpu.VMEM((slots, 5, 3, 2, LEVELS, LANES), f32),
            pltpu.VMEM((slots, 6, MARGIN, COLS), f32),
            pltpu.VMEM((8, WIDE, COLS + LANES), f32),
            pltpu.VMEM((4, 2, LEVELS * ROWS, LANES), f32),
            pltpu.VMEM((3, 2, ROWS, LANES), f32),
            dma((12,)),
            dma((11,)),
            dma((2, 2)),
            dma((2, 2)),
            dma((2, 2, 14)),
            dma((2, slots)),
            dma((2, 1, 2, slots)),
            dma((2, 1, 2, slots)),
        ],
        compiler_params=pltpu.CompilerParams(
            collective_id=collective_id, has_side_effects=True, vmem_limit_bytes=40 << 20
        ),
        name="ocean_step",
    )


def on_device(lon_size, lat_size, *arguments):
    *fields, sea, zon, mer, tally, seam = arguments
    deep = [x.reshape(LEVELS * ROWS, COLS) for x in fields]
    turn = lax.rem(seam[0] // COLS + lax.axis_index("lon"), lon_size)
    branches = [step_call(lon_size, lat_size, n, n) for n in range(lon_size)]
    out = lax.switch(turn, branches, seam, *deep, sea, zon, mer, tally)
    return tuple(x.reshape(LEVELS, ROWS, COLS) for x in out[:4]) + tuple(out[4:])


def solution(mesh):
    deep = P(None, "lat", "lon")
    flat = P("lat", "lon")
    return jax.shard_map(
        functools.partial(on_device, mesh.shape["lon"], mesh.shape["lat"]),
        mesh=mesh,
        in_specs=(deep,) * 4 + (flat,) * 4 + (P("lon"),),
        out_specs=(deep,) * 4 + (flat,) * 3,
        check_vma=False,
    )
```

```python
import functools

import jax
import jax.numpy as jnp
from jax import lax
from jax.experimental import pallas as pl
from jax.experimental.pallas import tpu as pltpu
from jax.sharding import PartitionSpec as P

MESH = pl.DeviceIdType.MESH

SUBSTEPS = 12
COURANT = 0.15
PRESSURE_GAIN = 0.1
CORIOLIS = 0.3
WAVE_MASS = 1.2
WAVE_MOMENTUM = 1.2
EPSILON = 1e-06

LEVELS, ROWS, COLS = 8, 16, 256
MARGIN = 2 * SUBSTEPS
WIDE = ROWS + 2 * MARGIN
LANES = 128

SEA, ZON, MER, TALLY, MEANZ, MEANM = range(6)


def weno_flux(em2, em1, e0, ep1, ep2, q0, q1, carry, drift, ahead):
    far = jnp.where(ahead, em2, ep2)
    near = jnp.where(ahead, em1, ep1)
    down = jnp.where(ahead, ep1, em1)
    centre = jnp.where(ahead, q0, q1)
    b0 = far * (4.0 * far - 11.0 * near) + (10.0 * near * near + 3.0 * EPSILON)
    b1 = near * (4.0 * near - 5.0 * e0) + (4.0 * e0 * e0 + 3.0 * EPSILON)
    b2 = e0 * (10.0 * e0 - 11.0 * down) + (4.0 * down * down + 3.0 * EPSILON)
    m0 = b1 * b2
    m1 = b0 * b2
    m2 = b0 * b1
    s0 = m0 * m0
    s1 = 6.0 * (m1 * m1)
    s2 = 3.0 * (m2 * m2)
    top = s0 * (5.0 * near - 2.0 * far) + s1 * (near + 2.0 * e0) + s2 * (4.0 * e0 - down)
    return carry * centre + drift * (top / (s0 + s1 + s2))


def wrapped(value, size):
    return lax.rem(value + 2 * size, size)


def turner(seam_ref):
    lane = lax.broadcasted_iota(jnp.int32, (LEVELS, LANES), 1)
    level = lax.broadcasted_iota(jnp.int32, (LEVELS, LANES), 0)
    first_partner = jnp.full((LEVELS, LANES), seam_ref[0], jnp.int32)
    upper = jnp.bitwise_and(first_partner, LANES) != 0
    base = jnp.bitwise_and(first_partner, LANES - 1)
    picked = jnp.bitwise_and(base - lane, LANES - 1)

    def turn_lanes(low, high):
        return jnp.take_along_axis(jnp.where(upper, high, low), picked, axis=1)

    mirror = LEVELS - 1 - level

    def flip_rows(x):
        return jnp.take_along_axis(x, mirror, axis=0)

    return turn_lanes, flip_rows, lane <= base


def pack_margins(tiles):
    lane = lax.broadcasted_iota(jnp.int32, (LEVELS, LANES), 1)
    group = lax.shift_right_logical(lane * 43, 10)
    west = jnp.zeros((LEVELS, LANES), jnp.float32)
    east = west
    for g, (first, last) in enumerate(tiles):
        if g:
            first = pltpu.roll(first, MARGIN * g, 1)
        last = pltpu.roll(last, (MARGIN * g + MARGIN) % LANES, 1)
        west = jnp.where(group == g, first, west)
        east = jnp.where(group == g, last, east)
    return west, east


def prepare(
    u_in, v_in, t_in, s_in, sea_in, zon_in, mer_in, tally_in, cells, edges, rim, margins,
    raw, tally_raw, flat, sems
):
    f32 = jnp.float32
    loads = [pltpu.make_async_copy(tally_in, tally_raw, sems.at[11])]
    for f, ref in enumerate((u_in, v_in, t_in, s_in)):
        for t in range(2):
            lanes = slice(t * LANES, (t + 1) * LANES)
            loads.append(pltpu.make_async_copy(ref.at[:, lanes], raw.at[f, t], sems.at[2 * f + t]))
    for f, ref in enumerate((sea_in, zon_in, mer_in)):
        loads.append(pltpu.make_async_copy(ref, rim.at[f], sems.at[8 + f]))
    for copy in loads:
        copy.start()
    for copy in loads:
        copy.wait()
    level = lax.broadcasted_iota(jnp.int32, (LEVELS, LANES), 0).astype(f32)
    lane = lax.broadcasted_iota(jnp.int32, (LEVELS, LANES), 1)
    for t in range(2):
        lanes = slice(t * LANES, (t + 1) * LANES)
        tally = tally_raw[:, lanes].astype(f32)
        rim[TALLY, :, lanes] = tally
        flat[t] = tally
    for pair in range(2):
        tiles = [
            (
                rim[2 * pair + g // 2, 8 * (g % 2) : 8 * (g % 2) + 8, 0:LANES],
                rim[2 * pair + g // 2, 8 * (g % 2) : 8 * (g % 2) + 8, LANES:COLS],
            )
            for g in range(4)
        ]
        margins[0, pair], margins[1, pair] = pack_margins(tiles)
    triple = lax.shift_right_logical(lane * 43, 7)
    for n in range(2):
        for f in range(5):
            edges[n, f] = jnp.zeros((LEVELS, LANES), f32)

    def arrange(r, _):
        mine = triple == r
        for f in range(5):
            tiles = []
            for t in range(2):
                if f < 4:
                    tile = raw[f, t, pl.ds(r, LEVELS, stride=ROWS), :]
                else:
                    tile = jnp.where(level < flat[t, pl.ds(r, 1), :], 1.0, 0.0)
                cells[f, r, t] = tile
                tiles.append(tile)
            edges[0, f] = jnp.where(mine, pltpu.roll(tiles[0], 3 * r, 1), edges[0, f])
            edges[1, f] = jnp.where(mine, pltpu.roll(tiles[1], 3 * r + 3, 1), edges[1, f])
        return _

    lax.fori_loop(0, ROWS, arrange, 0)


def prepare_call(*arguments):
    f32 = jnp.float32
    vmem = pl.BlockSpec(memory_space=pltpu.VMEM)
    anywhere = pl.BlockSpec(memory_space=pl.ANY)
    return pl.pallas_call(
        prepare,
        out_shape=(
            jax.ShapeDtypeStruct((5, ROWS, 2, LEVELS, LANES), f32),
            jax.ShapeDtypeStruct((2, 5, LEVELS, LANES), f32),
            jax.ShapeDtypeStruct((4, ROWS, COLS), f32),
            jax.ShapeDtypeStruct((2, 2, LEVELS, LANES), f32),
        ),
        in_specs=[anywhere] * 8,
        out_specs=(vmem,) * 4,
        scratch_shapes=[
            pltpu.VMEM((4, 2, LEVELS * ROWS, LANES), f32),
            pltpu.VMEM((ROWS, COLS), jnp.int32),
            pltpu.VMEM((2, ROWS, LANES), f32),
            pltpu.SemaphoreType.DMA((12,)),
        ],
        name="prepare",
    )(*arguments)


class Links:
    SHIFTS = [(a, b) for a in (1, -1, 2, -2, 0) for b in (0, 1, -1) if (a, b) != (0, 0)]

    def __init__(self, lon_size, lat_size, turn=None):
        self.lon = lax.axis_index("lon")
        self.lat = lax.axis_index("lat")
        self.lon_size, self.lat_size, self.turn = lon_size, lat_size, turn
        self.top = self.lat == lat_size - 1
        self.below = self.lat == lat_size - 2
        self.barrier = pltpu.get_barrier_semaphore()

    def fold_peer(self, s):
        return wrapped(self.turn - self.lon + s - 2, self.lon_size)

    def lat_ok(self, a):
        return jnp.logical_and(self.lat + a >= 0, self.lat + a <= self.lat_size - 1)

    def when_lat(self, a, body):
        if a == 0:
            body()
        else:
            pl.when(self.lat_ok(a))(body)

    def peer(self, a, b):
        return {"lat": self.lat + a, "lon": wrapped(self.lon + b, self.lon_size)}

    def greet(self, to):
        pl.semaphore_signal(self.barrier, inc=1, device_id=to, device_id_type=MESH)

    def meet(self, shifts, top_slots=(), below_slots=()):
        count = jnp.int32(0)
        for a, b in shifts:
            self.when_lat(a, lambda a=a, b=b: self.greet(self.peer(a, b)))
            count = count + (1 if a == 0 else self.lat_ok(a).astype(jnp.int32))
        fold_count = jnp.int32(len(below_slots))
        for s in top_slots:
            fold_count = fold_count + (self.fold_peer(s) != self.lon).astype(jnp.int32)
        if self.turn is not None:

            @pl.when(self.top)
            def _():
                for s in top_slots:
                    q = self.fold_peer(s)

                    @pl.when(q != self.lon)
                    def _():
                        self.greet({"lat": self.lat, "lon": q})

                for s in below_slots:
                    self.greet({"lat": self.lat - 1, "lon": self.fold_peer(s)})

            @pl.when(self.below)
            def _():
                for s in below_slots:
                    self.greet({"lat": self.lat + 1, "lon": self.fold_peer(s)})

            count = count + jnp.where(self.top, fold_count, 0)
            count = count + jnp.where(self.below, len(below_slots), 0)
        return count

    def copy(self, src, dst, sems, to):
        return pltpu.make_async_remote_copy(
            src_ref=src,
            dst_ref=dst,
            send_sem=sems.at[0],
            recv_sem=sems.at[1],
            device_id=to,
            device_id_type=MESH,
        )

    def rim_copy(self, n, own, margins, centre, blocks, sems):
        a, b = self.SHIFTS[n]
        to = self.peer(a, b)
        if b:
            side = 1 if b == 1 else 0
            return self.copy(margins.at[side], blocks.at[2 - a, side], sems.at[:, n], to)
        src_rows, dst_rows = {
            1: ((0, 16), (8, 24)),
            2: ((8, 16), (0, 8)),
            -1: ((0, 16), (MARGIN + 16, MARGIN + 32)),
            -2: ((0, 8), (MARGIN + 32, MARGIN + 40)),
        }[a]
        return self.copy(
            own.at[:, src_rows[0] : src_rows[1]],
            centre.at[:, dst_rows[0] : dst_rows[1]],
            sems.at[:, n],
            to,
        )

    def fold_start(self, s, copy, src, dst, sem, same_lat):
        if not same_lat:
            copy().start()
            return
        own = self.fold_peer(s) == self.lon

        @pl.when(jnp.logical_not(own))
        def _():
            copy().start()

        @pl.when(own)
        def _():
            pltpu.make_async_copy(src, dst, sem).start()

    def fold_sent(self, s, copy, same_lat):
        if not same_lat:
            copy().wait_send()
            return

        @pl.when(self.fold_peer(s) != self.lon)
        def _():
            copy().wait_send()

    def fold_rim_ref(self, kind, s, src, dst):
        rows = (0, 16) if kind == 0 else (8, 16)
        to = {0: (0, 16), 1: (8, 16), 2: (16, 24)}[kind]
        lanes = slice(*{0: (128, 256), 3: (0, 128)}.get(s, (0, 256)))
        slot = s - (4 - dst.shape[0]) // 2
        return src.at[:, rows[0] : rows[1], lanes], dst.at[slot, :, to[0] : to[1], lanes]

    def fold_rim_copy(self, kind, s, src, dst, sems):
        a, b = self.fold_rim_ref(kind, s, src, dst)
        to = {"lat": self.lat + (0, -1, 1)[kind], "lon": self.fold_peer(s)}
        return self.copy(a, b, sems.at[:, 0 if kind == 0 else 1, s], to)

    def fold_rim_kinds(self, slots, kinds, body):
        @pl.when(self.top)
        def _():
            for s in slots:
                for kind in (0, 1):
                    if kind in kinds:
                        body(kind, s)

        @pl.when(self.below)
        def _():
            for s in slots:
                body(2, s)

    def fold_rim_start(self, slots, kinds, src, dst, sems):
        def body(kind, s):
            a, b = self.fold_rim_ref(kind, s, src, dst)
            self.fold_start(
                s,
                lambda: self.fold_rim_copy(kind, s, src, dst, sems),
                a,
                b,
                sems.at[1, 0, s],
                kind == 0,
            )

        self.fold_rim_kinds(slots, kinds, body)

    def fold_rim_finish(self, slots, kinds, src, dst, sems):
        @pl.when(self.top)
        def _():
            for s in slots:
                self.fold_rim_copy(0, s, src, dst, sems).wait_recv()
                self.fold_rim_copy(2, s, src, dst, sems).wait_recv()

        if 1 in kinds:

            @pl.when(self.below)
            def _():
                for s in slots:
                    self.fold_rim_copy(1, s, src, dst, sems).wait_recv()

        self.fold_rim_kinds(
            slots,
            kinds,
            lambda kind, s: self.fold_sent(
                s, lambda: self.fold_rim_copy(kind, s, src, dst, sems), kind == 0
            ),
        )


def first_exchange(
    lon_size, lat_size, turn, cells, edges, rim, bands, edges_in, fold_cells, fold_rim,
    edge_sem, band_sem, wet_sem, fold_sem, fold_wet_sem, fold_rim_sem
):
    links = Links(lon_size, lat_size, turn)
    count = links.meet([(1, 0), (-1, 0), (0, 1), (0, -1)], (1, 2), (1, 2))
    pl.semaphore_wait(links.barrier, count)

    def edge_copy(side):
        return links.copy(
            edges.at[side], edges_in.at[side], edge_sem.at[:, side], links.peer(0, 2 * side - 1)
        )

    def band_copies(side):
        first = ROWS - 3 if side == 0 else 0
        wet_from, wet_to = (ROWS - 1, 2) if side == 0 else (0, 0)
        to = links.peer(1 - 2 * side, 0)
        return (
            links.copy(
                cells.at[0:4, first : first + 3], bands.at[side, 0:4], band_sem.at[:, side], to
            ),
            links.copy(cells.at[4, wet_from], bands.at[side, 4, wet_to], wet_sem.at[:, side], to),
        )

    fold_parts = (
        lambda s: (cells.at[0:4, ROWS - 3 : ROWS], fold_cells.at[s - 1, 0:4], fold_sem.at[:, s - 1]),
        lambda s: (cells.at[4, ROWS - 1], fold_cells.at[s - 1, 4, 2], fold_wet_sem.at[:, s - 1]),
    )

    def fold_cell_copy(s, part):
        return links.copy(*part(s), {"lat": links.lat, "lon": links.fold_peer(s)})

    @pl.when(links.top)
    def _():
        for s in (1, 2):
            for part in fold_parts:
                a, b, sem = part(s)
                links.fold_start(
                    s, lambda s=s, part=part: fold_cell_copy(s, part), a, b, sem.at[1], True
                )

    for side in range(2):

        def send(side=side):
            for copy in band_copies(side):
                copy.start()

        links.when_lat(1 - 2 * side, send)
    for side in range(2):
        edge_copy(side).start()
    links.fold_rim_start((1, 2), (0, 2), rim, fold_rim, fold_rim_sem)

    for side in range(2):
        edge_copy(side).wait()
    for side in range(2):

        def arrived(side=side):
            for copy in band_copies(side):
                copy.wait_recv()

        def sent(side=side):
            for copy in band_copies(side):
                copy.wait_send()

        links.when_lat(2 * side - 1, arrived)
        links.when_lat(1 - 2 * side, sent)

    @pl.when(links.top)
    def _():
        for s in (1, 2):
            for part in fold_parts:
                fold_cell_copy(s, part).wait_recv()
                links.fold_sent(s, lambda s=s, part=part: fold_cell_copy(s, part), True)

    links.fold_rim_finish((1, 2), (0, 2), rim, fold_rim, fold_rim_sem)


def first_exchange_call(lon_size, lat_size, turn, collective_id):
    f32 = jnp.float32
    anywhere = pl.BlockSpec(memory_space=pl.ANY)
    dma = pltpu.SemaphoreType.DMA
    return pl.pallas_call(
        functools.partial(first_exchange, lon_size, lat_size, turn),
        out_shape=(
            jax.ShapeDtypeStruct((2, 5, 3, 2, LEVELS, LANES), f32),
            jax.ShapeDtypeStruct((2, 5, LEVELS, LANES), f32),
            jax.ShapeDtypeStruct((2, 5, 3, 2, LEVELS, LANES), f32),
            jax.ShapeDtypeStruct((2, 4, MARGIN, COLS), f32),
        ),
        in_specs=[anywhere] * 3,
        out_specs=(anywhere,) * 4,
        scratch_shapes=[dma((2, 2))] * 5 + [dma((2, 2, 4))],
        compiler_params=pltpu.CompilerParams(collective_id=collective_id, has_side_effects=True),
        name="first_exchange",
    )


def interior(
    lon_size, lat_size, seam_ref, cells_in, edges, rim_in, bands, edges_in, fold_cells, fold_rim, rim_own, margins,
    centre, blocks, moved, done, means, mean_margins,
    cells, halo, face_west, flux_north, part, sums, ghost, ghost_margins, cell_sem, rim_sem, ghost_sem
):
    f32 = jnp.float32
    links = Links(lon_size, lat_size)
    lat = links.lat
    count = links.meet(Links.SHIFTS)
    filled = pltpu.make_async_copy(cells_in, cells.at[:, 3 : 3 + ROWS], cell_sem.at[0])
    south = pltpu.make_async_copy(bands.at[0], cells.at[:, 0:3], cell_sem.at[1])
    north = pltpu.make_async_copy(bands.at[1], cells.at[:, ROWS + 3 : ROWS + 6], cell_sem.at[2])
    keep = pltpu.make_async_copy(
        rim_own, centre.at[:, MARGIN : MARGIN + ROWS], cell_sem.at[3]
    )
    fold_in = pltpu.make_async_copy(ghost, centre.at[:, MARGIN + ROWS : WIDE], cell_sem.at[4])
    filled.start()
    keep.start()
    links.when_lat(-1, south.start)
    links.when_lat(1, north.start)

    @pl.when(lat == 0)
    def _():
        cells[:, 0:3] = jnp.zeros((5, 3, 2, LEVELS, LANES), f32)

    level = lax.broadcasted_iota(jnp.int32, (LEVELS, LANES), 0)
    lane = lax.broadcasted_iota(jnp.int32, (LEVELS, LANES), 1)

    @pl.when(links.top)
    def _():
        turn_lanes, flip_rows, same_tile = turner(seam_ref)

        def image(tile):
            turned = [turn_lanes(tile(2 - n), tile(3 - n)) for n in range(3)]
            return [jnp.where(same_tile, turned[t], turned[t + 1]) for t in range(2)]

        def across(g, _):
            for f in range(4):
                for t, value in enumerate(image(lambda n: fold_cells[n // 2, f, 2 - g, n % 2])):
                    cells[f, ROWS + 3 + g, t] = -value if f < 2 else value
            return _

        lax.fori_loop(0, 3, across, 0)
        for t, value in enumerate(image(lambda n: fold_cells[n // 2, 4, 2, n % 2])):
            cells[4, ROWS + 3, t] = value

        def across_rim(f, _):
            sign = jnp.where(jnp.logical_or(f == SEA, f == TALLY), 1.0, -1.0)
            for q, first in enumerate((8, 0, 16)):

                def tile(n):
                    lanes = slice((n % 2) * LANES, (n % 2 + 1) * LANES)
                    return fold_rim[n // 2, f, first : first + 8, lanes]

                for t, value in enumerate(image(tile)):
                    ghost[f, 8 * q : 8 * q + 8, t * LANES : (t + 1) * LANES] = flip_rows(value) * sign
            return _

        lax.fori_loop(0, 4, across_rim, 0)
        fold_in.start()
        for block in range(2):
            for pair in range(2):
                tiles = []
                for g in range(4):
                    first = 8 * (g % 2) if block == 0 else 16
                    rows = slice(first, first + 8)
                    f = 2 * pair + g // 2
                    tiles.append((ghost[f, rows, 0:LANES], ghost[f, rows, LANES:COLS]))
                packed = pack_margins(tiles)
                for side in range(2):
                    ghost_margins[block, side, pair] = packed[side]

    def ghost_copies(row):
        for side in range(2):
            to = links.peer(-row, 2 * side - 1)
            if row == 0:
                yield links.copy(
                    ghost_margins.at[:, side], blocks.at[3:5, side], ghost_sem.at[:, side], to
                )
            else:
                yield links.copy(
                    ghost_margins.at[0, side], blocks.at[4, side], ghost_sem.at[:, 2 + side], to
                )
        if row:
            yield links.copy(
                ghost.at[:, 0:8],
                centre.at[:, MARGIN + 32 : WIDE],
                ghost_sem.at[:, 4],
                links.peer(-1, 0),
            )

    def back(x, n):
        return pltpu.roll(x, LANES - n, 1)

    packed = []
    for f in range(5):
        west = edges_in[1, f]
        own = edges[0, f]
        packed.append((west, own))
    speed = 0.5 * (back(packed[0][0], 2) + packed[0][1]) * back(packed[4][0], 2) * packed[4][1]
    face_west[4] = speed
    for f in range(4):
        west, own = packed[f]
        inner = back(west, 2)
        ew = back(west, 1) - west
        eo = back(own, 1) - own
        face_west[f] = weno_flux(
            ew,
            back(ew, 1),
            own - inner,
            eo,
            back(eo, 1),
            inner,
            own,
            COURANT * speed,
            (COURANT / 6.0) * jnp.abs(speed),
            speed >= 0.0,
        )

    filled.wait()

    def north_face(face):
        speeds = []
        for t in range(2):
            speed = (
                0.5
                * (cells[1, face + 2, t] + cells[1, face + 3, t])
                * cells[4, face + 2, t]
                * cells[4, face + 3, t]
            )
            flux_north[4, face, t] = speed
            speeds.append(
                (COURANT * speed, (COURANT / 6.0) * jnp.abs(speed), speed >= 0.0)
            )
        for f in range(4):
            for t in range(2):
                q = [cells[f, face + n, t] for n in range(6)]
                e = [q[n + 1] - q[n] for n in range(5)]
                flux_north[f, face, t] = weno_flux(*e, q[2], q[3], *speeds[t])

    def north_loop(face, _):
        north_face(face)
        return _

    lax.fori_loop(3, 14, north_loop, 0)

    def rim_copy(n):
        return links.rim_copy(n, rim_own, margins, centre, blocks, rim_sem)

    pl.semaphore_wait(links.barrier, count)
    for n, (a, b) in enumerate(Links.SHIFTS):
        links.when_lat(a, lambda n=n: rim_copy(n).start())

    @pl.when(links.top)
    def _():
        for row in range(2):
            for copy in ghost_copies(row):
                copy.start()

    first_lane = lane == 0
    last_lane = lane == LANES - 1

    def unpack(r, _):
        for f in range(5):
            east = pltpu.roll(edges_in[0, f], LANES - 3 * r, 1)
            west = pltpu.roll(edges_in[1, f], LANES - 3 - 3 * r, 1)
            halo[f, r] = jnp.where(lane < LANES // 2, east, west)
        return _

    lax.fori_loop(0, ROWS, unpack, 0)

    def ahead_1(x):
        turned = [pltpu.roll(v, LANES - 1, 1) for v in x]
        return [jnp.where(last_lane, turned[(n + 1) % 3], turned[n]) for n in range(3)]

    def ahead_2(x):
        turned = [pltpu.roll(v, LANES - 2, 1) for v in x]
        return [
            jnp.where(lane >= LANES - 2, turned[(n + 1) % 3], turned[n]) for n in range(2)
        ]

    def behind_1(x):
        turned = [pltpu.roll(v, 1, 1) for v in x]
        return [jnp.where(first_lane, turned[(n + 2) % 3], turned[n]) for n in range(2)]

    def behind_2(x):
        turned = [pltpu.roll(v, 2, 1) for v in x]
        return [jnp.where(lane < 2, turned[(n + 2) % 3], turned[n]) for n in range(2)]

    def east_loop(r, _):
        wet = [cells[4, r + 3, 0], cells[4, r + 3, 1], halo[4, r]]
        wet_next = ahead_1(wet)
        gaps, nexts, firsts = [], [], []
        for f in range(4):
            q = [cells[f, r + 3, 0], cells[f, r + 3, 1], halo[f, r]]
            nxt = ahead_1(q)
            firsts.append(q)
            nexts.append(nxt)
            gaps.append([nxt[n] - q[n] for n in range(3)])
        speeds = []
        for t in range(2):
            speed = 0.5 * (firsts[0][t] + nexts[0][t]) * wet[t] * wet_next[t]
            speeds.append(speed)
        behind = []

        def difference(x, first):
            turned = [pltpu.roll(v, 1, 1) for v in x]
            return (
                x[0] - jnp.where(first_lane, first, turned[0]),
                x[1] - jnp.where(first_lane, turned[0], turned[1]),
            )

        def west_of(f):
            return pltpu.roll(face_west[f], LANES - 3 * r, 1)

        spread = difference(speeds, west_of(4))
        for t in range(2):
            part[4, r, t] = spread[t]
        for f in range(4):
            e = gaps[f]
            em1 = behind_1(e)
            em2 = behind_2(e)
            ep1 = ahead_1(e)
            ep2 = ahead_2(e)
            behind.append(em1)
            flux = [
                weno_flux(
                    em2[t],
                    em1[t],
                    e[t],
                    ep1[t],
                    ep2[t],
                    firsts[f][t],
                    nexts[f][t],
                    COURANT * speeds[t],
                    (COURANT / 6.0) * jnp.abs(speeds[t]),
                    speeds[t] >= 0.0,
                )
                for t in range(2)
            ]
            lost = difference(flux, west_of(f))
            for t in range(2):
                part[f, r, t] = lost[t]
        for t in range(2):
            part[5, r, t] = 0.8 * (gaps[3][t] + behind[3][t]) - 0.2 * (
                gaps[2][t] + behind[2][t]
            )
        return _

    lax.fori_loop(0, ROWS, east_loop, 0)

    links.when_lat(-1, south.wait)
    links.when_lat(1, north.wait)

    def outer_loop(n, _):
        north_face(n)
        north_face(n + 14)
        return _

    lax.fori_loop(0, 3, outer_loop, 0)

    def down_sum(x):
        for s in (1, 2, 4):
            x = x + jnp.where(level >= s, pltpu.roll(x, s, 0), 0.0)
        return x

    def up_sum(x):
        for s in (1, 2, 4):
            x = x + jnp.where(level < LEVELS - s, pltpu.roll(x, LEVELS - s, 0), 0.0)
        return x

    total_rows = ROWS * lat_size

    def combine(r, _):
        row = (lat * ROWS + r).astype(f32)
        coriolis = CORIOLIS * (2.0 * (row + 0.5) / total_rows - 1.0)
        for t in range(2):
            q = [cells[f, r + 3, t] for f in range(4)]
            wet = cells[4, r + 3, t]
            spread = part[4, r, t] + (flux_north[4, r + 1, t] - flux_north[4, r, t])
            lift = jnp.where(level >= 1, (-0.5 * COURANT) * up_sum(spread), 0.0)
            rates = []
            for f in range(4):
                vertical = lift * (pltpu.roll(q[f], 1, 0) + q[f])
                rates.append(
                    (pltpu.roll(vertical, LEVELS - 1, 0) - vertical)
                    - part[f, r, t]
                    - (flux_north[f, r + 1, t] - flux_north[f, r, t])
                )
            slope_east = part[5, r, t]
            slope_north = 0.8 * (cells[3, r + 4, t] - cells[3, r + 2, t]) - 0.2 * (
                cells[2, r + 4, t] - cells[2, r + 2, t]
            )
            grad_east = 0.5 * (down_sum(slope_east) - 0.5 * slope_east)
            grad_north = 0.5 * (down_sum(slope_north) - 0.5 * slope_north)
            force_zonal = rates[0] + coriolis * q[1] - PRESSURE_GAIN * grad_east
            force_merid = rates[1] - coriolis * q[0] - PRESSURE_GAIN * grad_north
            sums[0, t, pl.ds(r, 1), :] = jnp.sum(wet * force_zonal, axis=0, keepdims=True)
            sums[1, t, pl.ds(r, 1), :] = jnp.sum(wet * force_merid, axis=0, keepdims=True)
            moved[0, r, t] = q[0] + force_zonal
            moved[1, r, t] = q[1] + force_merid
            done[0, t, pl.ds(r, LEVELS, stride=ROWS), :] = wet * (q[2] + rates[2])
            done[1, t, pl.ds(r, LEVELS, stride=ROWS), :] = wet * (q[3] + rates[3])
        return _

    lax.fori_loop(0, ROWS, combine, 0)

    for t in range(2):
        lanes = slice(t * LANES, (t + 1) * LANES)
        column = jnp.maximum(rim_in[TALLY, :, lanes], 1.0)
        for f in range(2):
            sums[f, t] = sums[f, t] / column
            means[f, :, lanes] = sums[f, t]
    tiles = []
    for g in range(4):
        rows = slice(8 * (g % 2), 8 * (g % 2) + 8)
        tiles.append((sums[g // 2, 0, rows, :], sums[g // 2, 1, rows, :]))
    mean_margins[0, 0], mean_margins[1, 0] = pack_margins(tiles)

    keep.wait()
    for n, (a, b) in enumerate(Links.SHIFTS):
        links.when_lat(-a, lambda n=n: rim_copy(n).wait_recv())
    for n, (a, b) in enumerate(Links.SHIFTS):
        links.when_lat(a, lambda n=n: rim_copy(n).wait_send())

    @pl.when(links.top)
    def _():
        fold_in.wait()
        for copy in ghost_copies(0):
            copy.wait_recv()
        for row in range(2):
            for copy in ghost_copies(row):
                copy.wait_send()

    @pl.when(links.below)
    def _():
        for copy in ghost_copies(1):
            copy.wait_recv()


def interior_call(lon_size, lat_size, collective_id):
    f32 = jnp.float32
    vmem = pl.BlockSpec(memory_space=pltpu.VMEM)
    anywhere = pl.BlockSpec(memory_space=pl.ANY)
    dma = pltpu.SemaphoreType.DMA
    return pl.pallas_call(
        functools.partial(interior, lon_size, lat_size),
        out_shape=(
            jax.ShapeDtypeStruct((4, WIDE, COLS), f32),
            jax.ShapeDtypeStruct((5, 2, 2, LEVELS, LANES), f32),
            jax.ShapeDtypeStruct((2, ROWS, 2, LEVELS, LANES), f32),
            jax.ShapeDtypeStruct((2, 2, LEVELS * ROWS, LANES), f32),
            jax.ShapeDtypeStruct((2, ROWS, COLS), f32),
            jax.ShapeDtypeStruct((2, 1, LEVELS, LANES), f32),
        ),
        in_specs=[pl.BlockSpec(memory_space=pltpu.SMEM)]
        + [anywhere, vmem, vmem, anywhere, vmem, vmem, vmem, anywhere, anywhere],
        out_specs=(anywhere, anywhere, vmem, vmem, vmem, vmem),
        scratch_shapes=[
            pltpu.VMEM((5, ROWS + 6, 2, LEVELS, LANES), f32),
            pltpu.VMEM((5, ROWS, LEVELS, LANES), f32),
            pltpu.VMEM((5, LEVELS, LANES), f32),
            pltpu.VMEM((5, ROWS + 1, 2, LEVELS, LANES), f32),
            pltpu.VMEM((6, ROWS, 2, LEVELS, LANES), f32),
            pltpu.VMEM((2, 2, ROWS, LANES), f32),
            pltpu.VMEM((4, MARGIN, COLS), f32),
            pltpu.VMEM((2, 2, 2, LEVELS, LANES), f32),
            dma((5,)),
            dma((2, 14)),
            dma((2, 5)),
        ],
        compiler_params=pltpu.CompilerParams(collective_id=collective_id, has_side_effects=True),
        name="interior",
    )


def second_exchange(
    lon_size, lat_size, turn, means, margins, centre, blocks, fold_rim, rim_sem, fold_rim_sem
):
    links = Links(lon_size, lat_size, turn)
    count = links.meet(Links.SHIFTS, (0, 1, 2, 3), (0, 1, 2, 3))
    pl.semaphore_wait(links.barrier, count)
    slots, kinds = (0, 1, 2, 3), (0, 1, 2)

    def rim_copy(n):
        return links.rim_copy(n, means, margins, centre, blocks, rim_sem)

    links.fold_rim_start(slots, kinds, means, fold_rim, fold_rim_sem)
    for n, (a, b) in enumerate(Links.SHIFTS):
        links.when_lat(a, lambda n=n: rim_copy(n).start())
    for n, (a, b) in enumerate(Links.SHIFTS):
        links.when_lat(-a, lambda n=n: rim_copy(n).wait_recv())
    links.fold_rim_finish(slots, kinds, means, fold_rim, fold_rim_sem)
    for n, (a, b) in enumerate(Links.SHIFTS):
        links.when_lat(a, lambda n=n: rim_copy(n).wait_send())


def second_exchange_call(lon_size, lat_size, turn, collective_id):
    f32 = jnp.float32
    anywhere = pl.BlockSpec(memory_space=pl.ANY)
    dma = pltpu.SemaphoreType.DMA
    return pl.pallas_call(
        functools.partial(second_exchange, lon_size, lat_size, turn),
        out_shape=(
            jax.ShapeDtypeStruct((2, WIDE, COLS), f32),
            jax.ShapeDtypeStruct((5, 2, 1, LEVELS, LANES), f32),
            jax.ShapeDtypeStruct((4, 2, MARGIN, COLS), f32),
        ),
        in_specs=[anywhere] * 2,
        out_specs=(anywhere,) * 3,
        scratch_shapes=[dma((2, 14)), dma((2, 2, 4))],
        compiler_params=pltpu.CompilerParams(collective_id=collective_id, has_side_effects=True),
        name="second_exchange",
    )


def finish(
    lat_size, seam_ref, centre_a, blocks_a, centre_b, blocks_b, fold_b, means, rim_own, moved, done_in,
    u_out, v_out, t_out, s_out, sea_out, zon_out, mer_out,
    wave, done, flat, tally, sems
):
    f32 = jnp.float32
    lat = lax.axis_index("lat")
    total_rows = ROWS * lat_size
    width = COLS + LANES
    stores = []
    for f, ref in ((2, t_out), (3, s_out)):
        for t in range(2):
            lanes = slice(t * LANES, (t + 1) * LANES)
            stores.append(pltpu.make_async_copy(done_in.at[f - 2, t], ref.at[:, lanes], sems.at[2 * f + t]))
    for copy in stores:
        copy.start()

    lane = lax.broadcasted_iota(jnp.int32, (LEVELS, LANES), 1)
    own_rows = slice(MARGIN, MARGIN + ROWS)
    row = lax.broadcasted_iota(jnp.int32, (WIDE, width), 0) + (lat * ROWS - MARGIN)
    sources = ((0, 1), (1, 0), (1, 1), (2, 0), (2, 1), (3, 0), (3, 1), (4, 0))
    for f in range(6):
        centre, blocks, n = (centre_a, blocks_a, f) if f < 4 else (centre_b, blocks_b, f - 4)
        wave[f, :, 0:COLS] = centre[n]
        for i, (block, part) in enumerate(sources):
            lead = MARGIN * (2 * (n % 2) + part)
            from_east = blocks[block, 0, n // 2]
            if lead:
                from_east = pltpu.roll(from_east, LANES - lead, 1)
            from_west = pltpu.roll(blocks[block, 1, n // 2], LANES - MARGIN - lead, 1)
            wave[f, 8 * i : 8 * i + 8, COLS:width] = jnp.where(
                lane < LANES // 2, from_east, from_west
            )
    for f in range(2):
        wave[MEANZ + f, own_rows, 0:COLS] = means[f]
    for n, empty in ((0, MARGIN), (1, 8)):

        @pl.when(lat == n)
        def _():
            wave[0:6, 0:empty] = jnp.zeros((6, empty, width), f32)

    def unfold(ghost_tiles):
        turn_lanes, flip_rows, same_tile = turner(seam_ref)

        def mean(n, _):
            for to, source in ghost_tiles:

                def tile(m):
                    at = slice((m % 2) * LANES, (m % 2 + 1) * LANES)
                    return fold_b[m // 2, n, source : source + 8, at]

                turned = {m: turn_lanes(tile(m + 4), tile(m + 5)) for m in range(-3, 2)}
                image = {
                    m: -flip_rows(jnp.where(same_tile, turned[m], turned[m - 1]))
                    for m in range(-2, 2)
                }
                f = n + MEANZ
                wave[f, to : to + 8, 0:128] = image[0]
                wave[f, to : to + 8, 128:256] = image[-1]
                wave[f, to : to + 8, 256:384] = jnp.where(lane < LANES // 2, image[-2], image[1])
            return _

        lax.fori_loop(0, 2, mean, 0)

    pl.when(lat == lat_size - 1)(lambda: unfold(((40, 8), (48, 0), (56, 16))))
    pl.when(lat == lat_size - 2)(lambda: unfold(((56, 8),)))

    mirrored = jnp.minimum(row, 2 * total_rows - 1 - row).astype(f32)
    wide_tally = wave[TALLY]
    wave[6] = jnp.where(wide_tally > 0.0, 1.0, 0.0)
    wave[TALLY] = wide_tally * (0.5 * WAVE_MASS / LEVELS)
    wave[7] = (CORIOLIS / SUBSTEPS) * (2.0 * (mirrored + 0.5) / total_rows - 1.0)
    wave[MEANZ] = wave[MEANZ] * (1.0 / SUBSTEPS)
    wave[MEANM] = wave[MEANM] * (1.0 / SUBSTEPS)

    def east_difference(x):
        return pltpu.roll(x, width - 1, 1) - pltpu.roll(x, 1, 1)

    def north_difference(x):
        return pltpu.roll(x, WIDE - 1, 0) - pltpu.roll(x, 1, 0)

    def substep(n, _):
        thick = wave[TALLY]
        wet = wave[6]
        zonal = wave[ZON]
        merid = wave[MER]
        level_next = wet * (
            wave[SEA] - (east_difference(thick * zonal) + north_difference(thick * merid))
        )
        turn_rate = wave[7]
        wave[SEA] = level_next
        wave[ZON] = wet * (
            zonal
            - (0.5 * WAVE_MOMENTUM) * east_difference(level_next)
            + (turn_rate * merid + wave[MEANZ])
        )
        wave[MER] = wet * (
            merid
            - (0.5 * WAVE_MOMENTUM) * north_difference(level_next)
            + (wave[MEANM] - turn_rate * zonal)
        )
        return _

    lax.fori_loop(0, SUBSTEPS, substep, 0)

    for f, ref in enumerate((sea_out, zon_out, mer_out)):
        copy = pltpu.make_async_copy(wave.at[f, own_rows, 0:COLS], ref, sems.at[8 + f])
        copy.start()
        stores.append(copy)
    for t in range(2):
        lanes = slice(t * LANES, (t + 1) * LANES)
        tally[t] = rim_own[TALLY, :, lanes]
        for f in range(2):
            flat[f, t] = wave[ZON + f, own_rows, lanes] - rim_own[ZON + f, :, lanes] - means[f, :, lanes]
    level = lax.broadcasted_iota(jnp.int32, (LEVELS, LANES), 0).astype(f32)

    def last(r, _):
        for t in range(2):
            wet = level < tally[t, pl.ds(r, 1), :]
            for f in range(2):
                shift = flat[f, t, pl.ds(r, 1), :]
                done[f, t, pl.ds(r, LEVELS, stride=ROWS), :] = jnp.where(
                    wet, moved[f, r, t] + shift, 0.0
                )
        return _

    lax.fori_loop(0, ROWS, last, 0)

    for f, ref in ((0, u_out), (1, v_out)):
        for t in range(2):
            lanes = slice(t * LANES, (t + 1) * LANES)
            copy = pltpu.make_async_copy(done.at[f, t], ref.at[:, lanes], sems.at[2 * f + t])
            copy.start()
            stores.append(copy)
    for copy in stores:
        copy.wait()


def finish_call(lat_size, *arguments):
    f32 = jnp.float32
    deep = jax.ShapeDtypeStruct((LEVELS * ROWS, COLS), f32)
    flat = jax.ShapeDtypeStruct((ROWS, COLS), f32)
    vmem = pl.BlockSpec(memory_space=pltpu.VMEM)
    anywhere = pl.BlockSpec(memory_space=pl.ANY)
    return pl.pallas_call(
        functools.partial(finish, lat_size),
        out_shape=(deep,) * 4 + (flat,) * 3,
        in_specs=[pl.BlockSpec(memory_space=pltpu.SMEM)] + [vmem] * 9,
        out_specs=(anywhere,) * 7,
        scratch_shapes=[
            pltpu.VMEM((8, WIDE, COLS + LANES), f32),
            pltpu.VMEM((2, 2, LEVELS * ROWS, LANES), f32),
            pltpu.VMEM((2, 2, ROWS, LANES), f32),
            pltpu.VMEM((2, ROWS, LANES), f32),
            pltpu.SemaphoreType.DMA((11,)),
        ],
        name="finish",
    )(*arguments)


def on_device(lon_size, lat_size, *arguments):
    *fields, sea, zon, mer, tally, seam = arguments
    deep = [x.reshape(LEVELS * ROWS, COLS) for x in fields]
    turn = lax.rem(lax.shift_right_logical(seam[0], 8) + lax.axis_index("lon"), lon_size)
    cells, edges, rim_own, margins = prepare_call(*deep, sea, zon, mer, tally)
    bands, edges_in, fold_cells, fold_a = lax.switch(
        turn,
        [first_exchange_call(lon_size, lat_size, n, n) for n in range(lon_size)],
        cells,
        edges,
        rim_own,
    )
    centre_a, blocks_a, moved, done, means, mean_margins = interior_call(
        lon_size, lat_size, 2 * lon_size
    )(seam, cells, edges, rim_own, bands, edges_in, fold_cells, fold_a, rim_own, margins)
    centre_b, blocks_b, fold_b = lax.switch(
        turn,
        [second_exchange_call(lon_size, lat_size, n, lon_size + n) for n in range(lon_size)],
        means,
        mean_margins,
    )
    out = finish_call(
        lat_size, seam, centre_a, blocks_a, centre_b, blocks_b, fold_b, means, rim_own, moved, done
    )
    return tuple(x.reshape(LEVELS, ROWS, COLS) for x in out[:4]) + tuple(out[4:])


def solution(mesh):
    deep = P(None, "lat", "lon")
    flat = P("lat", "lon")
    return jax.shard_map(
        functools.partial(on_device, mesh.shape["lon"], mesh.shape["lat"]),
        mesh=mesh,
        in_specs=(deep,) * 4 + (flat,) * 4 + (P("lon"),),
        out_specs=(deep,) * 4 + (flat,) * 3,
        check_vma=False,
    )
```

```python
import functools

import jax
import jax.numpy as jnp
from jax import lax
from jax.experimental import pallas as pl
from jax.experimental.pallas import tpu as pltpu
from jax.sharding import PartitionSpec as P

MESH = pl.DeviceIdType.MESH

SUBSTEPS = 12
COURANT = 0.15
PRESSURE_GAIN = 0.1
CORIOLIS = 0.3
WAVE_MASS = 1.2
WAVE_MOMENTUM = 1.2
EPSILON = 1e-06

LEVELS, ROWS, COLS = 8, 16, 256
MARGIN = 2 * SUBSTEPS
WIDE = ROWS + 2 * MARGIN
LANES = 128

SEA, ZON, MER, TALLY, MEANZ, MEANM = range(6)


def weno_flux(em2, em1, e0, ep1, ep2, q0, q1, carry, drift, ahead):
    far = jnp.where(ahead, em2, ep2)
    near = jnp.where(ahead, em1, ep1)
    down = jnp.where(ahead, ep1, em1)
    centre = jnp.where(ahead, q0, q1)
    b0 = far * (4.0 * far - 11.0 * near) + (10.0 * near * near + 3.0 * EPSILON)
    b1 = near * (4.0 * near - 5.0 * e0) + (4.0 * e0 * e0 + 3.0 * EPSILON)
    b2 = e0 * (10.0 * e0 - 11.0 * down) + (4.0 * down * down + 3.0 * EPSILON)
    m0 = b1 * b2
    m1 = b0 * b2
    m2 = b0 * b1
    s0 = m0 * m0
    s1 = 6.0 * (m1 * m1)
    s2 = 3.0 * (m2 * m2)
    top = s0 * (5.0 * near - 2.0 * far) + s1 * (near + 2.0 * e0) + s2 * (4.0 * e0 - down)
    return carry * centre + drift * (top / (s0 + s1 + s2))


def wrapped(value, size):
    return lax.rem(value + 2 * size, size)


def turner(fold_ref):
    lane = lax.broadcasted_iota(jnp.int32, (LEVELS, LANES), 1)
    level = lax.broadcasted_iota(jnp.int32, (LEVELS, LANES), 0)
    first_partner = jnp.full((LEVELS, LANES), fold_ref[1], jnp.int32)
    upper = jnp.bitwise_and(first_partner, LANES) != 0
    base = jnp.bitwise_and(first_partner, LANES - 1)
    picked = jnp.bitwise_and(base - lane, LANES - 1)

    def turn_lanes(low, high):
        return jnp.take_along_axis(jnp.where(upper, high, low), picked, axis=1)

    mirror = LEVELS - 1 - level

    def flip_rows(x):
        return jnp.take_along_axis(x, mirror, axis=0)

    return turn_lanes, flip_rows, lane <= base


def pack_margins(tiles):
    lane = lax.broadcasted_iota(jnp.int32, (LEVELS, LANES), 1)
    group = lax.shift_right_logical(lane * 43, 10)
    west = jnp.zeros((LEVELS, LANES), jnp.float32)
    east = west
    for g, (first, last) in enumerate(tiles):
        if g:
            first = pltpu.roll(first, MARGIN * g, 1)
        last = pltpu.roll(last, (MARGIN * g + MARGIN) % LANES, 1)
        west = jnp.where(group == g, first, west)
        east = jnp.where(group == g, last, east)
    return west, east


def prepare(
    lon_size, u_in, v_in, t_in, s_in, sea_in, zon_in, mer_in, tally_in, seam_in, cells, edges, rim, margins, fold,
    raw, tally_raw, flat, seam, sems
):
    f32 = jnp.float32
    loads = [
        pltpu.make_async_copy(seam_in, seam, sems.at[12]),
        pltpu.make_async_copy(tally_in, tally_raw, sems.at[11]),
    ]
    for f, ref in enumerate((u_in, v_in, t_in, s_in)):
        for t in range(2):
            lanes = slice(t * LANES, (t + 1) * LANES)
            loads.append(pltpu.make_async_copy(ref.at[:, lanes], raw.at[f, t], sems.at[2 * f + t]))
    for f, ref in enumerate((sea_in, zon_in, mer_in)):
        loads.append(pltpu.make_async_copy(ref, rim.at[f], sems.at[8 + f]))
    for copy in loads:
        copy.start()
    for copy in loads:
        copy.wait()
    fold[0] = lax.rem(lax.shift_right_logical(seam[0], 8) + lax.axis_index("lon"), lon_size)
    fold[1] = seam[0]
    level = lax.broadcasted_iota(jnp.int32, (LEVELS, LANES), 0).astype(f32)
    lane = lax.broadcasted_iota(jnp.int32, (LEVELS, LANES), 1)
    for t in range(2):
        lanes = slice(t * LANES, (t + 1) * LANES)
        tally = tally_raw[:, lanes].astype(f32)
        rim[TALLY, :, lanes] = tally
        flat[t] = tally
    for pair in range(2):
        tiles = [
            (
                rim[2 * pair + g // 2, 8 * (g % 2) : 8 * (g % 2) + 8, 0:LANES],
                rim[2 * pair + g // 2, 8 * (g % 2) : 8 * (g % 2) + 8, LANES:COLS],
            )
            for g in range(4)
        ]
        margins[0, pair], margins[1, pair] = pack_margins(tiles)
    triple = lax.shift_right_logical(lane * 43, 7)
    for n in range(2):
        for f in range(5):
            edges[n, f] = jnp.zeros((LEVELS, LANES), f32)

    def arrange(r, _):
        mine = triple == r
        for f in range(5):
            tiles = []
            for t in range(2):
                if f < 4:
                    tile = raw[f, t, pl.ds(r, LEVELS, stride=ROWS), :]
                else:
                    tile = jnp.where(level < flat[t, pl.ds(r, 1), :], 1.0, 0.0)
                cells[f, r, t] = tile
                tiles.append(tile)
            edges[0, f] = jnp.where(mine, pltpu.roll(tiles[0], 3 * r, 1), edges[0, f])
            edges[1, f] = jnp.where(mine, pltpu.roll(tiles[1], 3 * r + 3, 1), edges[1, f])
        return _

    lax.fori_loop(0, ROWS, arrange, 0, unroll=16)


def prepare_call(lon_size, *arguments):
    f32 = jnp.float32
    vmem = pl.BlockSpec(memory_space=pltpu.VMEM)
    anywhere = pl.BlockSpec(memory_space=pl.ANY)
    return pl.pallas_call(
        functools.partial(prepare, lon_size),
        out_shape=(
            jax.ShapeDtypeStruct((5, ROWS, 2, LEVELS, LANES), f32),
            jax.ShapeDtypeStruct((2, 5, LEVELS, LANES), f32),
            jax.ShapeDtypeStruct((4, ROWS, COLS), f32),
            jax.ShapeDtypeStruct((2, 2, LEVELS, LANES), f32),
            jax.ShapeDtypeStruct((2,), jnp.int32),
        ),
        in_specs=[anywhere] * 9,
        out_specs=(vmem,) * 4 + (pl.BlockSpec(memory_space=pltpu.SMEM),),
        scratch_shapes=[
            pltpu.VMEM((4, 2, LEVELS * ROWS, LANES), f32),
            pltpu.VMEM((ROWS, COLS), jnp.int32),
            pltpu.VMEM((2, ROWS, LANES), f32),
            pltpu.SMEM((COLS,), jnp.int32),
            pltpu.SemaphoreType.DMA((13,)),
        ],
        name="prepare",
    )(*arguments)


class Links:
    SHIFTS = [(a, b) for a in (1, -1, 2, -2, 0) for b in (0, 1, -1) if (a, b) != (0, 0)]
    NEAR = [n for n, (a, b) in enumerate(SHIFTS) if abs(a) < 2]
    FAR = [n for n, (a, b) in enumerate(SHIFTS) if abs(a) == 2]

    def __init__(self, lon_size, lat_size, turn=None):
        self.lon = lax.axis_index("lon")
        self.lat = lax.axis_index("lat")
        self.lon_size, self.lat_size, self.turn = lon_size, lat_size, turn
        self.top = self.lat == lat_size - 1
        self.below = self.lat == lat_size - 2
        self.barrier = pltpu.get_barrier_semaphore()

    def fold_peer(self, s):
        return wrapped(self.turn - self.lon + s - 2, self.lon_size)

    def lat_ok(self, a):
        return jnp.logical_and(self.lat + a >= 0, self.lat + a <= self.lat_size - 1)

    def when_lat(self, a, body):
        if a == 0:
            body()
        else:
            pl.when(self.lat_ok(a))(body)

    def peer(self, a, b):
        return {"lat": self.lat + a, "lon": wrapped(self.lon + b, self.lon_size)}

    def greet(self, to):
        pl.semaphore_signal(self.barrier, inc=1, device_id=to, device_id_type=MESH)

    def meet(self, shifts, top_slots=(), below_slots=()):
        count = jnp.int32(0)
        for a, b in shifts:
            self.when_lat(a, lambda a=a, b=b: self.greet(self.peer(a, b)))
            count = count + (1 if a == 0 else self.lat_ok(a).astype(jnp.int32))
        fold_count = jnp.int32(len(below_slots))
        for s in top_slots:
            fold_count = fold_count + (self.fold_peer(s) != self.lon).astype(jnp.int32)
        if self.turn is not None:

            @pl.when(self.top)
            def _():
                for s in top_slots:
                    q = self.fold_peer(s)

                    @pl.when(q != self.lon)
                    def _():
                        self.greet({"lat": self.lat, "lon": q})

                for s in below_slots:
                    self.greet({"lat": self.lat - 1, "lon": self.fold_peer(s)})

            @pl.when(self.below)
            def _():
                for s in below_slots:
                    self.greet({"lat": self.lat + 1, "lon": self.fold_peer(s)})

            count = count + jnp.where(self.top, fold_count, 0)
            count = count + jnp.where(self.below, len(below_slots), 0)
        return count

    def copy(self, src, dst, sems, to):
        return pltpu.make_async_remote_copy(
            src_ref=src,
            dst_ref=dst,
            send_sem=sems.at[0],
            recv_sem=sems.at[1],
            device_id=to,
            device_id_type=MESH,
        )

    def rim_copy(self, n, own, margins, centre, blocks, sems):
        a, b = self.SHIFTS[n]
        to = self.peer(a, b)
        if b:
            side = 1 if b == 1 else 0
            return self.copy(margins.at[side], blocks.at[2 - a, side], sems.at[:, n], to)
        src_rows, dst_rows = {
            1: ((0, 16), (8, 24)),
            2: ((8, 16), (0, 8)),
            -1: ((0, 16), (MARGIN + 16, MARGIN + 32)),
            -2: ((0, 8), (MARGIN + 32, MARGIN + 40)),
        }[a]
        return self.copy(
            own.at[:, src_rows[0] : src_rows[1]],
            centre.at[:, dst_rows[0] : dst_rows[1]],
            sems.at[:, n],
            to,
        )

    def far_copy(self, n, own, margins, rows, blocks, sems):
        a, b = self.SHIFTS[n]
        to = self.peer(a, b)
        side = 0 if a > 0 else 1
        if b:
            edge = 1 if b == 1 else 0
            return self.copy(margins.at[edge], blocks.at[side, edge], sems.at[:, n], to)
        src = slice(8, 16) if a > 0 else slice(0, 8)
        return self.copy(own.at[:, src], rows.at[side], sems.at[:, n], to)

    def fold_start(self, s, copy, src, dst, sem, same_lat):
        if not same_lat:
            copy().start()
            return
        own = self.fold_peer(s) == self.lon

        @pl.when(jnp.logical_not(own))
        def _():
            copy().start()

        @pl.when(own)
        def _():
            pltpu.make_async_copy(src, dst, sem).start()

    def fold_sent(self, s, copy, same_lat):
        if not same_lat:
            copy().wait_send()
            return

        @pl.when(self.fold_peer(s) != self.lon)
        def _():
            copy().wait_send()

    def fold_rim_ref(self, kind, s, src, dst):
        rows = (0, 16) if kind == 0 else (8, 16)
        to = {0: (0, 16), 1: (8, 16), 2: (16, 24)}[kind]
        lanes = slice(*{0: (128, 256), 3: (0, 128)}.get(s, (0, 256)))
        slot = s - (4 - dst.shape[0]) // 2
        return src.at[:, rows[0] : rows[1], lanes], dst.at[slot, :, to[0] : to[1], lanes]

    def fold_rim_copy(self, kind, s, src, dst, sems):
        a, b = self.fold_rim_ref(kind, s, src, dst)
        to = {"lat": self.lat + (0, -1, 1)[kind], "lon": self.fold_peer(s)}
        return self.copy(a, b, sems.at[:, 0 if kind == 0 else 1, s], to)

    def fold_rim_kinds(self, slots, kinds, body):
        @pl.when(self.top)
        def _():
            for s in slots:
                for kind in (0, 1):
                    if kind in kinds:
                        body(kind, s)

        @pl.when(self.below)
        def _():
            for s in slots:
                body(2, s)

    def fold_rim_start(self, slots, kinds, src, dst, sems):
        def body(kind, s):
            a, b = self.fold_rim_ref(kind, s, src, dst)
            self.fold_start(
                s,
                lambda: self.fold_rim_copy(kind, s, src, dst, sems),
                a,
                b,
                sems.at[1, 0, s],
                kind == 0,
            )

        self.fold_rim_kinds(slots, kinds, body)

    def fold_rim_finish(self, slots, kinds, src, dst, sems):
        @pl.when(self.top)
        def _():
            for s in slots:
                self.fold_rim_copy(0, s, src, dst, sems).wait_recv()
                self.fold_rim_copy(2, s, src, dst, sems).wait_recv()

        if 1 in kinds:

            @pl.when(self.below)
            def _():
                for s in slots:
                    self.fold_rim_copy(1, s, src, dst, sems).wait_recv()

        self.fold_rim_kinds(
            slots,
            kinds,
            lambda kind, s: self.fold_sent(
                s, lambda: self.fold_rim_copy(kind, s, src, dst, sems), kind == 0
            ),
        )


def first_exchange(
    lon_size, lat_size, turn, cells, edges, rim, margins, bands, edges_in, fold_cells, fold_rim, far_rows, far_blocks,
    far_sem, edge_sem, band_sem, wet_sem, fold_sem, fold_wet_sem, fold_rim_sem
):
    links = Links(lon_size, lat_size, turn)
    far = [Links.SHIFTS[n] for n in Links.FAR]
    count = links.meet([(1, 0), (-1, 0), (0, 1), (0, -1)] + far, (1, 2), (1, 2))
    pl.semaphore_wait(links.barrier, count)

    def edge_copy(side):
        return links.copy(
            edges.at[side], edges_in.at[side], edge_sem.at[:, side], links.peer(0, 2 * side - 1)
        )

    def band_copies(side):
        first = ROWS - 3 if side == 0 else 0
        wet_from, wet_to = (ROWS - 1, 2) if side == 0 else (0, 0)
        to = links.peer(1 - 2 * side, 0)
        return (
            links.copy(
                cells.at[0:4, first : first + 3], bands.at[side, 0:4], band_sem.at[:, side], to
            ),
            links.copy(cells.at[4, wet_from], bands.at[side, 4, wet_to], wet_sem.at[:, side], to),
        )

    fold_parts = (
        lambda s: (cells.at[0:4, ROWS - 3 : ROWS], fold_cells.at[s - 1, 0:4], fold_sem.at[:, s - 1]),
        lambda s: (cells.at[4, ROWS - 1], fold_cells.at[s - 1, 4, 2], fold_wet_sem.at[:, s - 1]),
    )

    def fold_cell_copy(s, part):
        return links.copy(*part(s), {"lat": links.lat, "lon": links.fold_peer(s)})

    @pl.when(links.top)
    def _():
        for s in (1, 2):
            for part in fold_parts:
                a, b, sem = part(s)
                links.fold_start(
                    s, lambda s=s, part=part: fold_cell_copy(s, part), a, b, sem.at[1], True
                )

    for side in range(2):

        def send(side=side):
            for copy in band_copies(side):
                copy.start()

        links.when_lat(1 - 2 * side, send)
    for side in range(2):
        edge_copy(side).start()
    links.fold_rim_start((1, 2), (0, 2), rim, fold_rim, fold_rim_sem)

    def far_copy(n):
        return links.far_copy(n, rim, margins, far_rows, far_blocks, far_sem)

    for n in Links.FAR:
        links.when_lat(Links.SHIFTS[n][0], lambda n=n: far_copy(n).start())

    for side in range(2):
        edge_copy(side).wait()
    for side in range(2):

        def arrived(side=side):
            for copy in band_copies(side):
                copy.wait_recv()

        def sent(side=side):
            for copy in band_copies(side):
                copy.wait_send()

        links.when_lat(2 * side - 1, arrived)
        links.when_lat(1 - 2 * side, sent)

    @pl.when(links.top)
    def _():
        for s in (1, 2):
            for part in fold_parts:
                fold_cell_copy(s, part).wait_recv()
                links.fold_sent(s, lambda s=s, part=part: fold_cell_copy(s, part), True)

    links.fold_rim_finish((1, 2), (0, 2), rim, fold_rim, fold_rim_sem)
    for n in Links.FAR:
        links.when_lat(-Links.SHIFTS[n][0], lambda n=n: far_copy(n).wait_recv())
    for n in Links.FAR:
        links.when_lat(Links.SHIFTS[n][0], lambda n=n: far_copy(n).wait_send())


def first_exchange_call(lon_size, lat_size, turn, collective_id):
    f32 = jnp.float32
    anywhere = pl.BlockSpec(memory_space=pl.ANY)
    dma = pltpu.SemaphoreType.DMA
    return pl.pallas_call(
        functools.partial(first_exchange, lon_size, lat_size, turn),
        out_shape=(
            jax.ShapeDtypeStruct((2, 5, 3, 2, LEVELS, LANES), f32),
            jax.ShapeDtypeStruct((2, 5, LEVELS, LANES), f32),
            jax.ShapeDtypeStruct((2, 5, 3, 2, LEVELS, LANES), f32),
            jax.ShapeDtypeStruct((2, 4, MARGIN, COLS), f32),
            jax.ShapeDtypeStruct((2, 4, 8, COLS), f32),
            jax.ShapeDtypeStruct((2, 2, 2, LEVELS, LANES), f32),
        ),
        in_specs=[anywhere] * 4,
        out_specs=(anywhere,) * 6,
        scratch_shapes=[dma((2, 14))] + [dma((2, 2))] * 5 + [dma((2, 2, 4))],
        compiler_params=pltpu.CompilerParams(
            collective_id=collective_id, has_side_effects=True, vmem_limit_bytes=4 << 20
        ),
        name="first_exchange",
    )


def interior(
    lon_size, lat_size, fold_ref, cells_in, edges, rim_in, bands, edges_in, fold_cells, fold_rim, rim_own, margins,
    centre, blocks, moved, done, means, mean_margins,
    cells, halo, face_west, flux_north, part, sums, ghost, ghost_margins, cell_sem, rim_sem, ghost_sem
):
    f32 = jnp.float32
    links = Links(lon_size, lat_size)
    lat = links.lat
    near = [(n, Links.SHIFTS[n]) for n in Links.NEAR]
    count = links.meet([shift for _, shift in near])
    filled = pltpu.make_async_copy(cells_in, cells.at[:, 3 : 3 + ROWS], cell_sem.at[0])
    south = pltpu.make_async_copy(bands.at[0], cells.at[:, 0:3], cell_sem.at[1])
    north = pltpu.make_async_copy(bands.at[1], cells.at[:, ROWS + 3 : ROWS + 6], cell_sem.at[2])
    keep = pltpu.make_async_copy(
        rim_own, centre.at[:, MARGIN : MARGIN + ROWS], cell_sem.at[3]
    )
    fold_in = pltpu.make_async_copy(ghost, centre.at[:, MARGIN + ROWS : WIDE], cell_sem.at[4])
    filled.start()
    keep.start()
    links.when_lat(-1, south.start)
    links.when_lat(1, north.start)

    @pl.when(lat == 0)
    def _():
        cells[:, 0:3] = jnp.zeros((5, 3, 2, LEVELS, LANES), f32)

    level = lax.broadcasted_iota(jnp.int32, (LEVELS, LANES), 0)
    lane = lax.broadcasted_iota(jnp.int32, (LEVELS, LANES), 1)

    @pl.when(links.top)
    def _():
        turn_lanes, flip_rows, same_tile = turner(fold_ref)

        def image(tile):
            turned = [turn_lanes(tile(2 - n), tile(3 - n)) for n in range(3)]
            return [jnp.where(same_tile, turned[t], turned[t + 1]) for t in range(2)]

        def across(g, _):
            for f in range(4):
                for t, value in enumerate(image(lambda n: fold_cells[n // 2, f, 2 - g, n % 2])):
                    cells[f, ROWS + 3 + g, t] = -value if f < 2 else value
            return _

        lax.fori_loop(0, 3, across, 0)
        for t, value in enumerate(image(lambda n: fold_cells[n // 2, 4, 2, n % 2])):
            cells[4, ROWS + 3, t] = value

        def across_rim(f, _):
            sign = jnp.where(jnp.logical_or(f == SEA, f == TALLY), 1.0, -1.0)
            for q, first in enumerate((8, 0, 16)):

                def tile(n):
                    lanes = slice((n % 2) * LANES, (n % 2 + 1) * LANES)
                    return fold_rim[n // 2, f, first : first + 8, lanes]

                for t, value in enumerate(image(tile)):
                    ghost[f, 8 * q : 8 * q + 8, t * LANES : (t + 1) * LANES] = flip_rows(value) * sign
            return _

        lax.fori_loop(0, 4, across_rim, 0)
        fold_in.start()
        for block in range(2):
            for pair in range(2):
                tiles = []
                for g in range(4):
                    first = 8 * (g % 2) if block == 0 else 16
                    rows = slice(first, first + 8)
                    f = 2 * pair + g // 2
                    tiles.append((ghost[f, rows, 0:LANES], ghost[f, rows, LANES:COLS]))
                packed = pack_margins(tiles)
                for side in range(2):
                    ghost_margins[block, side, pair] = packed[side]

    def ghost_copies(row):
        for side in range(2):
            to = links.peer(-row, 2 * side - 1)
            if row == 0:
                yield links.copy(
                    ghost_margins.at[:, side], blocks.at[3:5, side], ghost_sem.at[:, side], to
                )
            else:
                yield links.copy(
                    ghost_margins.at[0, side], blocks.at[4, side], ghost_sem.at[:, 2 + side], to
                )
        if row:
            yield links.copy(
                ghost.at[:, 0:8],
                centre.at[:, MARGIN + 32 : WIDE],
                ghost_sem.at[:, 4],
                links.peer(-1, 0),
            )

    def back(x, n):
        return pltpu.roll(x, LANES - n, 1)

    packed = []
    for f in range(5):
        west = edges_in[1, f]
        own = edges[0, f]
        packed.append((west, own))
    speed = 0.5 * (back(packed[0][0], 2) + packed[0][1]) * back(packed[4][0], 2) * packed[4][1]
    face_west[4] = speed
    for f in range(4):
        west, own = packed[f]
        inner = back(west, 2)
        ew = back(west, 1) - west
        eo = back(own, 1) - own
        face_west[f] = weno_flux(
            ew,
            back(ew, 1),
            own - inner,
            eo,
            back(eo, 1),
            inner,
            own,
            COURANT * speed,
            (COURANT / 6.0) * jnp.abs(speed),
            speed >= 0.0,
        )


    def unpack(r, _):
        for f in range(5):
            east = pltpu.roll(edges_in[0, f], LANES - 3 * r, 1)
            west = pltpu.roll(edges_in[1, f], LANES - 3 - 3 * r, 1)
            halo[f, r] = jnp.where(lane < LANES // 2, east, west)
        return _

    lax.fori_loop(0, ROWS, unpack, 0, unroll=16)

    def rim_copy(n):
        return links.rim_copy(n, rim_own, margins, centre, blocks, rim_sem)

    pl.semaphore_wait(links.barrier, count)
    for n, (a, b) in near:
        links.when_lat(a, lambda n=n: rim_copy(n).start())

    @pl.when(links.top)
    def _():
        for row in range(2):
            for copy in ghost_copies(row):
                copy.start()

    def north_face(face, cells, first):
        def at(f, row, t):
            return cells[f, row - first, t]

        speeds = []
        for t in range(2):
            speed = (
                0.5
                * (at(1, face - 1, t) + at(1, face, t))
                * at(4, face - 1, t)
                * at(4, face, t)
            )
            flux_north[4, face, t] = speed
            speeds.append(
                (COURANT * speed, (COURANT / 6.0) * jnp.abs(speed), speed >= 0.0)
            )
        for f in range(4):
            for t in range(2):
                q = [at(f, face + n - 3, t) for n in range(6)]
                e = [q[n + 1] - q[n] for n in range(5)]
                flux_north[f, face, t] = weno_flux(*e, q[2], q[3], *speeds[t])

    def north_loop(face, _):
        north_face(face, cells_in, 0)
        return _

    lax.fori_loop(3, 14, north_loop, 0, unroll=11)

    def ahead(x, n, count=2):
        return [
            pltpu.roll(jnp.where(lane < n, x[(t + 1) % 3], x[t]), LANES - n, 1)
            for t in range(count)
        ]

    def behind(x, n):
        return [
            pltpu.roll(jnp.where(lane >= LANES - n, x[(t + 2) % 3], x[t]), n, 1) for t in range(2)
        ]

    def east_loop(r, _):
        wet = [cells_in[4, r, 0], cells_in[4, r, 1], halo[4, r]]
        wet_next = ahead(wet, 1)
        gaps, nexts, firsts = [], [], []
        for f in range(4):
            q = [cells_in[f, r, 0], cells_in[f, r, 1], halo[f, r]]
            nxt = ahead(q, 1, 3)
            firsts.append(q)
            nexts.append(nxt)
            gaps.append([nxt[n] - q[n] for n in range(3)])
        speeds = []
        for t in range(2):
            speed = 0.5 * (firsts[0][t] + nexts[0][t]) * wet[t] * wet_next[t]
            speeds.append(speed)
        trails = []

        def difference(x, first):
            west = behind([x[0], x[1], first], 1)
            return x[0] - west[0], x[1] - west[1]

        def west_of(f):
            return pltpu.roll(face_west[f], LANES - 1 - 3 * r, 1)

        spread = difference(speeds, west_of(4))
        for t in range(2):
            part[4, r, t] = spread[t]
        for f in range(4):
            e = gaps[f]
            em1 = behind(e, 1)
            em2 = behind(e, 2)
            ep1 = ahead(e, 1)
            ep2 = ahead(e, 2)
            trails.append(em1)
            flux = [
                weno_flux(
                    em2[t],
                    em1[t],
                    e[t],
                    ep1[t],
                    ep2[t],
                    firsts[f][t],
                    nexts[f][t],
                    COURANT * speeds[t],
                    (COURANT / 6.0) * jnp.abs(speeds[t]),
                    speeds[t] >= 0.0,
                )
                for t in range(2)
            ]
            lost = difference(flux, west_of(f))
            for t in range(2):
                part[f, r, t] = lost[t]
        for t in range(2):
            part[5, r, t] = 0.8 * (gaps[3][t] + trails[3][t]) - 0.2 * (
                gaps[2][t] + trails[2][t]
            )
        return _

    lax.fori_loop(0, ROWS, east_loop, 0, unroll=4)

    filled.wait()
    links.when_lat(-1, south.wait)
    links.when_lat(1, north.wait)

    def outer_loop(n, _):
        north_face(n, cells, -3)
        north_face(n + 14, cells, -3)
        return _

    lax.fori_loop(0, 3, outer_loop, 0)

    def down_sum(x):
        for s in (1, 2, 4):
            x = x + jnp.where(level >= s, pltpu.roll(x, s, 0), 0.0)
        return x

    def up_sum(x):
        for s in (1, 2, 4):
            x = x + jnp.where(level < LEVELS - s, pltpu.roll(x, LEVELS - s, 0), 0.0)
        return x

    total_rows = ROWS * lat_size

    def combine(r, _):
        row = (lat * ROWS + r).astype(f32)
        coriolis = CORIOLIS * (2.0 * (row + 0.5) / total_rows - 1.0)
        for t in range(2):
            q = [cells[f, r + 3, t] for f in range(4)]
            wet = cells[4, r + 3, t]
            spread = part[4, r, t] + (flux_north[4, r + 1, t] - flux_north[4, r, t])
            lift = jnp.where(level >= 1, (-0.5 * COURANT) * up_sum(spread), 0.0)
            rates = []
            for f in range(4):
                vertical = lift * (pltpu.roll(q[f], 1, 0) + q[f])
                rates.append(
                    (pltpu.roll(vertical, LEVELS - 1, 0) - vertical)
                    - part[f, r, t]
                    - (flux_north[f, r + 1, t] - flux_north[f, r, t])
                )
            slope_east = part[5, r, t]
            slope_north = 0.8 * (cells[3, r + 4, t] - cells[3, r + 2, t]) - 0.2 * (
                cells[2, r + 4, t] - cells[2, r + 2, t]
            )
            grad_east = 0.5 * (down_sum(slope_east) - 0.5 * slope_east)
            grad_north = 0.5 * (down_sum(slope_north) - 0.5 * slope_north)
            force_zonal = rates[0] + coriolis * q[1] - PRESSURE_GAIN * grad_east
            force_merid = rates[1] - coriolis * q[0] - PRESSURE_GAIN * grad_north
            sums[0, t, pl.ds(r, 1), :] = jnp.sum(wet * force_zonal, axis=0, keepdims=True)
            sums[1, t, pl.ds(r, 1), :] = jnp.sum(wet * force_merid, axis=0, keepdims=True)
            moved[0, r, t] = q[0] + force_zonal
            moved[1, r, t] = q[1] + force_merid
            done[0, t, pl.ds(r, LEVELS, stride=ROWS), :] = wet * (q[2] + rates[2])
            done[1, t, pl.ds(r, LEVELS, stride=ROWS), :] = wet * (q[3] + rates[3])
        return _

    lax.fori_loop(0, ROWS, combine, 0, unroll=4)

    for t in range(2):
        lanes = slice(t * LANES, (t + 1) * LANES)
        column = jnp.maximum(rim_in[TALLY, :, lanes], 1.0)
        for f in range(2):
            sums[f, t] = sums[f, t] / column
            means[f, :, lanes] = sums[f, t]
    tiles = []
    for g in range(4):
        rows = slice(8 * (g % 2), 8 * (g % 2) + 8)
        tiles.append((sums[g // 2, 0, rows, :], sums[g // 2, 1, rows, :]))
    mean_margins[0, 0], mean_margins[1, 0] = pack_margins(tiles)

    keep.wait()
    for n, (a, b) in near:
        links.when_lat(-a, lambda n=n: rim_copy(n).wait_recv())
    for n, (a, b) in near:
        links.when_lat(a, lambda n=n: rim_copy(n).wait_send())

    @pl.when(links.top)
    def _():
        fold_in.wait()
        for copy in ghost_copies(0):
            copy.wait_recv()
        for row in range(2):
            for copy in ghost_copies(row):
                copy.wait_send()

    @pl.when(links.below)
    def _():
        for copy in ghost_copies(1):
            copy.wait_recv()


def interior_call(lon_size, lat_size, collective_id):
    f32 = jnp.float32
    vmem = pl.BlockSpec(memory_space=pltpu.VMEM)
    anywhere = pl.BlockSpec(memory_space=pl.ANY)
    dma = pltpu.SemaphoreType.DMA
    return pl.pallas_call(
        functools.partial(interior, lon_size, lat_size),
        out_shape=(
            jax.ShapeDtypeStruct((4, WIDE, COLS), f32),
            jax.ShapeDtypeStruct((5, 2, 2, LEVELS, LANES), f32),
            jax.ShapeDtypeStruct((2, ROWS, 2, LEVELS, LANES), f32),
            jax.ShapeDtypeStruct((2, 2, LEVELS * ROWS, LANES), f32),
            jax.ShapeDtypeStruct((2, ROWS, COLS), f32),
            jax.ShapeDtypeStruct((2, 1, LEVELS, LANES), f32),
        ),
        in_specs=[pl.BlockSpec(memory_space=pltpu.SMEM)]
        + [vmem, vmem, vmem, anywhere, vmem, vmem, vmem, anywhere, anywhere],
        out_specs=(anywhere, anywhere, vmem, vmem, vmem, vmem),
        scratch_shapes=[
            pltpu.VMEM((5, ROWS + 6, 2, LEVELS, LANES), f32),
            pltpu.VMEM((5, ROWS, LEVELS, LANES), f32),
            pltpu.VMEM((5, LEVELS, LANES), f32),
            pltpu.VMEM((5, ROWS + 1, 2, LEVELS, LANES), f32),
            pltpu.VMEM((6, ROWS, 2, LEVELS, LANES), f32),
            pltpu.VMEM((2, 2, ROWS, LANES), f32),
            pltpu.VMEM((4, MARGIN, COLS), f32),
            pltpu.VMEM((2, 2, 2, LEVELS, LANES), f32),
            dma((5,)),
            dma((2, 14)),
            dma((2, 5)),
        ],
        compiler_params=pltpu.CompilerParams(
            collective_id=collective_id, has_side_effects=True, vmem_limit_bytes=12 << 20
        ),
        name="interior",
    )


def second_exchange(
    lon_size, lat_size, turn, means, margins, centre, blocks, fold_rim, rim_sem, fold_rim_sem
):
    links = Links(lon_size, lat_size, turn)
    count = links.meet(Links.SHIFTS, (0, 1, 2, 3), (0, 1, 2, 3))
    pl.semaphore_wait(links.barrier, count)
    slots, kinds = (0, 1, 2, 3), (0, 1, 2)

    def rim_copy(n):
        return links.rim_copy(n, means, margins, centre, blocks, rim_sem)

    links.fold_rim_start(slots, kinds, means, fold_rim, fold_rim_sem)
    for n, (a, b) in enumerate(Links.SHIFTS):
        links.when_lat(a, lambda n=n: rim_copy(n).start())
    for n, (a, b) in enumerate(Links.SHIFTS):
        links.when_lat(-a, lambda n=n: rim_copy(n).wait_recv())
    links.fold_rim_finish(slots, kinds, means, fold_rim, fold_rim_sem)
    for n, (a, b) in enumerate(Links.SHIFTS):
        links.when_lat(a, lambda n=n: rim_copy(n).wait_send())


def second_exchange_call(lon_size, lat_size, turn, collective_id):
    f32 = jnp.float32
    anywhere = pl.BlockSpec(memory_space=pl.ANY)
    dma = pltpu.SemaphoreType.DMA
    return pl.pallas_call(
        functools.partial(second_exchange, lon_size, lat_size, turn),
        out_shape=(
            jax.ShapeDtypeStruct((2, WIDE, COLS), f32),
            jax.ShapeDtypeStruct((5, 2, 1, LEVELS, LANES), f32),
            jax.ShapeDtypeStruct((4, 2, MARGIN, COLS), f32),
        ),
        in_specs=[anywhere] * 2,
        out_specs=(anywhere,) * 3,
        scratch_shapes=[dma((2, 14)), dma((2, 2, 4))],
        compiler_params=pltpu.CompilerParams(
            collective_id=collective_id, has_side_effects=True, vmem_limit_bytes=4 << 20
        ),
        name="second_exchange",
    )


def finish(
    lat_size, fold_ref, far_rows, far_blocks, centre_a, blocks_a, centre_b, blocks_b, fold_b, means, rim_own, moved, done_in,
    u_out, v_out, t_out, s_out, sea_out, zon_out, mer_out,
    wave, done, flat, tally, sems
):
    f32 = jnp.float32
    lat = lax.axis_index("lat")
    total_rows = ROWS * lat_size
    width = COLS + LANES
    stores = []
    for f, ref in ((2, t_out), (3, s_out)):
        for t in range(2):
            lanes = slice(t * LANES, (t + 1) * LANES)
            stores.append(pltpu.make_async_copy(done_in.at[f - 2, t], ref.at[:, lanes], sems.at[2 * f + t]))
    for copy in stores:
        copy.start()

    lane = lax.broadcasted_iota(jnp.int32, (LEVELS, LANES), 1)
    own_rows = slice(MARGIN, MARGIN + ROWS)
    row = lax.broadcasted_iota(jnp.int32, (WIDE, width), 0) + (lat * ROWS - MARGIN)

    def side_tile(from_east, from_west, n, part):
        lead = MARGIN * (2 * (n % 2) + part)
        if lead:
            from_east = pltpu.roll(from_east, LANES - lead, 1)
        from_west = pltpu.roll(from_west, LANES - MARGIN - lead, 1)
        return jnp.where(lane < LANES // 2, from_east, from_west)

    sources = ((0, 1), (1, 0), (1, 1), (2, 0), (2, 1), (3, 0), (3, 1), (4, 0))
    for f in range(6):
        centre, blocks, n = (centre_a, blocks_a, f) if f < 4 else (centre_b, blocks_b, f - 4)
        wave[f, :, 0:COLS] = centre[n]
        for i in range(8):
            block, part = sources[i]
            wave[f, 8 * i : 8 * i + 8, COLS:width] = side_tile(
                blocks[block, 0, n // 2], blocks[block, 1, n // 2], n, part
            )
    for side, rows, part, here in ((0, 0, 1, lat > 1), (1, WIDE - 8, 0, lat < lat_size - 2)):

        @pl.when(here)
        def _():
            for f in range(4):
                wave[f, rows : rows + 8, 0:COLS] = far_rows[side, f]
                wave[f, rows : rows + 8, COLS:width] = side_tile(
                    far_blocks[side, 0, f // 2], far_blocks[side, 1, f // 2], f, part
                )

    for f in range(2):
        wave[MEANZ + f, own_rows, 0:COLS] = means[f]
    for n, empty in ((0, MARGIN), (1, 8)):

        @pl.when(lat == n)
        def _():
            wave[0:6, 0:empty] = jnp.zeros((6, empty, width), f32)

    def unfold(ghost_tiles):
        turn_lanes, flip_rows, same_tile = turner(fold_ref)

        def mean(n, _):
            for to, source in ghost_tiles:

                def tile(m):
                    at = slice((m % 2) * LANES, (m % 2 + 1) * LANES)
                    return fold_b[m // 2, n, source : source + 8, at]

                turned = {m: turn_lanes(tile(m + 4), tile(m + 5)) for m in range(-3, 2)}
                image = {
                    m: -flip_rows(jnp.where(same_tile, turned[m], turned[m - 1]))
                    for m in range(-2, 2)
                }
                f = n + MEANZ
                wave[f, to : to + 8, 0:128] = image[0]
                wave[f, to : to + 8, 128:256] = image[-1]
                wave[f, to : to + 8, 256:384] = jnp.where(lane < LANES // 2, image[-2], image[1])
            return _

        lax.fori_loop(0, 2, mean, 0)

    pl.when(lat == lat_size - 1)(lambda: unfold(((40, 8), (48, 0), (56, 16))))
    pl.when(lat == lat_size - 2)(lambda: unfold(((56, 8),)))

    mirrored = jnp.minimum(row, 2 * total_rows - 1 - row).astype(f32)
    wide_tally = wave[TALLY]
    wave[6] = jnp.where(wide_tally > 0.0, 1.0, 0.0)
    wave[TALLY] = wide_tally * (0.5 * WAVE_MASS / LEVELS)
    wave[7] = (CORIOLIS / SUBSTEPS) * (2.0 * (mirrored + 0.5) / total_rows - 1.0)
    wave[MEANZ] = wave[MEANZ] * (1.0 / SUBSTEPS)
    wave[MEANM] = wave[MEANM] * (1.0 / SUBSTEPS)

    def east_difference(x):
        return pltpu.roll(x, width - 1, 1) - pltpu.roll(x, 1, 1)

    def north_difference(x):
        return pltpu.roll(x, x.shape[0] - 1, 0) - pltpu.roll(x, 1, 0)

    def substep(rows):
        thick = wave[TALLY, rows]
        wet = wave[6, rows]
        zonal = wave[ZON, rows]
        merid = wave[MER, rows]
        level_next = wet * (
            wave[SEA, rows] - (east_difference(thick * zonal) + north_difference(thick * merid))
        )
        turn_rate = wave[7, rows]
        wave[SEA, rows] = level_next
        wave[ZON, rows] = wet * (
            zonal
            - (0.5 * WAVE_MOMENTUM) * east_difference(level_next)
            + (turn_rate * merid + wave[MEANZ, rows])
        )
        wave[MER, rows] = wet * (
            merid
            - (0.5 * WAVE_MOMENTUM) * north_difference(level_next)
            + (wave[MEANM, rows] - turn_rate * zonal)
        )

    for stage in range(SUBSTEPS // 4):
        rows = slice(8 * stage, WIDE - 8 * stage)
        lax.fori_loop(0, 4, lambda n, _: (substep(rows), _)[1], 0)

    for f, ref in enumerate((sea_out, zon_out, mer_out)):
        copy = pltpu.make_async_copy(wave.at[f, own_rows, 0:COLS], ref, sems.at[8 + f])
        copy.start()
        stores.append(copy)
    for t in range(2):
        lanes = slice(t * LANES, (t + 1) * LANES)
        tally[t] = rim_own[TALLY, :, lanes]
        for f in range(2):
            flat[f, t] = wave[ZON + f, own_rows, lanes] - rim_own[ZON + f, :, lanes] - means[f, :, lanes]
    level = lax.broadcasted_iota(jnp.int32, (LEVELS, LANES), 0).astype(f32)

    def last(r, _):
        for t in range(2):
            wet = level < tally[t, pl.ds(r, 1), :]
            for f in range(2):
                shift = flat[f, t, pl.ds(r, 1), :]
                done[f, t, pl.ds(r, LEVELS, stride=ROWS), :] = jnp.where(
                    wet, moved[f, r, t] + shift, 0.0
                )
        return _

    lax.fori_loop(0, ROWS, last, 0, unroll=16)

    for f, ref in ((0, u_out), (1, v_out)):
        for t in range(2):
            lanes = slice(t * LANES, (t + 1) * LANES)
            copy = pltpu.make_async_copy(done.at[f, t], ref.at[:, lanes], sems.at[2 * f + t])
            copy.start()
            stores.append(copy)
    for copy in stores:
        copy.wait()


def finish_call(lat_size, *arguments):
    f32 = jnp.float32
    deep = jax.ShapeDtypeStruct((LEVELS * ROWS, COLS), f32)
    flat = jax.ShapeDtypeStruct((ROWS, COLS), f32)
    vmem = pl.BlockSpec(memory_space=pltpu.VMEM)
    anywhere = pl.BlockSpec(memory_space=pl.ANY)
    return pl.pallas_call(
        functools.partial(finish, lat_size),
        out_shape=(deep,) * 4 + (flat,) * 3,
        in_specs=[pl.BlockSpec(memory_space=pltpu.SMEM)] + [vmem] * 11,
        out_specs=(anywhere,) * 7,
        scratch_shapes=[
            pltpu.VMEM((8, WIDE, COLS + LANES), f32),
            pltpu.VMEM((2, 2, LEVELS * ROWS, LANES), f32),
            pltpu.VMEM((2, 2, ROWS, LANES), f32),
            pltpu.VMEM((2, ROWS, LANES), f32),
            pltpu.SemaphoreType.DMA((11,)),
        ],
        compiler_params=pltpu.CompilerParams(vmem_limit_bytes=12 << 20),
        name="finish",
    )(*arguments)


def on_device(lon_size, lat_size, *arguments):
    *fields, sea, zon, mer, tally, seam = arguments
    deep = [x.reshape(LEVELS * ROWS, COLS) for x in fields]
    cells, edges, rim_own, margins, fold = prepare_call(lon_size, *deep, sea, zon, mer, tally, seam)
    turn = fold[0]
    bands, edges_in, fold_cells, fold_a, far_rows, far_blocks = lax.switch(
        turn,
        [first_exchange_call(lon_size, lat_size, n, n) for n in range(lon_size)],
        cells,
        edges,
        rim_own,
        margins,
    )
    centre_a, blocks_a, moved, done, means, mean_margins = interior_call(
        lon_size, lat_size, 2 * lon_size
    )(fold, cells, edges, rim_own, bands, edges_in, fold_cells, fold_a, rim_own, margins)
    centre_b, blocks_b, fold_b = lax.switch(
        turn,
        [second_exchange_call(lon_size, lat_size, n, lon_size + n) for n in range(lon_size)],
        means,
        mean_margins,
    )
    out = finish_call(
        lat_size, fold, far_rows, far_blocks, centre_a, blocks_a, centre_b, blocks_b, fold_b, means, rim_own,
        moved, done
    )
    return tuple(x.reshape(LEVELS, ROWS, COLS) for x in out[:4]) + tuple(out[4:])


def solution(mesh):
    deep = P(None, "lat", "lon")
    flat = P("lat", "lon")
    return jax.shard_map(
        functools.partial(on_device, mesh.shape["lon"], mesh.shape["lat"]),
        mesh=mesh,
        in_specs=(deep,) * 4 + (flat,) * 4 + (P("lon"),),
        out_specs=(deep,) * 4 + (flat,) * 3,
        check_vma=False,
    )
```

```python
import functools

import jax
import jax.numpy as jnp
from jax import lax
from jax.experimental import pallas as pl
from jax.experimental.pallas import tpu as pltpu
from jax.sharding import PartitionSpec as P

MESH = pl.DeviceIdType.MESH

SUBSTEPS = 12
COURANT = 0.15
PRESSURE_GAIN = 0.1
CORIOLIS = 0.3
WAVE_MASS = 1.2
WAVE_MOMENTUM = 1.2
EPSILON = 1e-06

LEVELS, ROWS, COLS = 8, 16, 256
MARGIN = 2 * SUBSTEPS
WIDE = ROWS + 2 * MARGIN
LANES = 128

SEA, ZON, MER, TALLY, MEANZ, MEANM = range(6)


def weno_flux(em2, em1, e0, ep1, ep2, q0, q1, carry, drift, ahead):
    far = jnp.where(ahead, em2, ep2)
    near = jnp.where(ahead, em1, ep1)
    down = jnp.where(ahead, ep1, em1)
    centre = jnp.where(ahead, q0, q1)
    b0 = far * (4.0 * far - 11.0 * near) + (10.0 * near * near + 3.0 * EPSILON)
    b1 = near * (4.0 * near - 5.0 * e0) + (4.0 * e0 * e0 + 3.0 * EPSILON)
    b2 = e0 * (10.0 * e0 - 11.0 * down) + (4.0 * down * down + 3.0 * EPSILON)
    m0 = b1 * b2
    m1 = b0 * b2
    m2 = b0 * b1
    s0 = m0 * m0
    s1 = 6.0 * (m1 * m1)
    s2 = 3.0 * (m2 * m2)
    top = s0 * (5.0 * near - 2.0 * far) + s1 * (near + 2.0 * e0) + s2 * (4.0 * e0 - down)
    return carry * centre + drift * (top / (s0 + s1 + s2))


def wrapped(value, size):
    return lax.rem(value + 2 * size, size)


def turner(fold_ref):
    lane = lax.broadcasted_iota(jnp.int32, (LEVELS, LANES), 1)
    level = lax.broadcasted_iota(jnp.int32, (LEVELS, LANES), 0)
    first_partner = jnp.full((LEVELS, LANES), fold_ref[1], jnp.int32)
    upper = jnp.bitwise_and(first_partner, LANES) != 0
    base = jnp.bitwise_and(first_partner, LANES - 1)
    picked = jnp.bitwise_and(base - lane, LANES - 1)

    def turn_lanes(low, high):
        return jnp.take_along_axis(jnp.where(upper, high, low), picked, axis=1)

    mirror = LEVELS - 1 - level

    def flip_rows(x):
        return jnp.take_along_axis(x, mirror, axis=0)

    return turn_lanes, flip_rows, lane <= base


def pack_margins(tiles):
    lane = lax.broadcasted_iota(jnp.int32, (LEVELS, LANES), 1)
    group = lax.shift_right_logical(lane * 43, 10)
    west = jnp.zeros((LEVELS, LANES), jnp.float32)
    east = west
    for g, (first, last) in enumerate(tiles):
        if g:
            first = pltpu.roll(first, MARGIN * g, 1)
        last = pltpu.roll(last, (MARGIN * g + MARGIN) % LANES, 1)
        west = jnp.where(group == g, first, west)
        east = jnp.where(group == g, last, east)
    return west, east


def prepare(
    lon_size, u_in, v_in, t_in, s_in, sea_in, zon_in, mer_in, tally_in, seam_in, cells, edges, rim, margins, fold,
    raw, tally_raw, flat, seam, sems
):
    f32 = jnp.float32
    loads = [
        pltpu.make_async_copy(seam_in, seam, sems.at[12]),
        pltpu.make_async_copy(tally_in, tally_raw, sems.at[11]),
    ]
    for f, ref in enumerate((u_in, v_in, t_in, s_in)):
        for t in range(2):
            lanes = slice(t * LANES, (t + 1) * LANES)
            loads.append(pltpu.make_async_copy(ref.at[:, lanes], raw.at[f, t], sems.at[2 * f + t]))
    for f, ref in enumerate((sea_in, zon_in, mer_in)):
        loads.append(pltpu.make_async_copy(ref, rim.at[f], sems.at[8 + f]))
    for copy in loads:
        copy.start()
    for copy in loads:
        copy.wait()
    fold[0] = lax.rem(lax.shift_right_logical(seam[0], 8) + lax.axis_index("lon"), lon_size)
    fold[1] = seam[0]
    level = lax.broadcasted_iota(jnp.int32, (LEVELS, LANES), 0).astype(f32)
    lane = lax.broadcasted_iota(jnp.int32, (LEVELS, LANES), 1)
    for t in range(2):
        lanes = slice(t * LANES, (t + 1) * LANES)
        tally = tally_raw[:, lanes].astype(f32)
        rim[TALLY, :, lanes] = tally
        flat[t] = tally
    for pair in range(2):
        tiles = [
            (
                rim[2 * pair + g // 2, 8 * (g % 2) : 8 * (g % 2) + 8, 0:LANES],
                rim[2 * pair + g // 2, 8 * (g % 2) : 8 * (g % 2) + 8, LANES:COLS],
            )
            for g in range(4)
        ]
        margins[0, pair], margins[1, pair] = pack_margins(tiles)
    triple = lax.shift_right_logical(lane * 43, 7)
    for n in range(2):
        for f in range(5):
            edges[n, f] = jnp.zeros((LEVELS, LANES), f32)

    def arrange(r, _):
        mine = triple == r
        for f in range(5):
            tiles = []
            for t in range(2):
                if f < 4:
                    tile = raw[f, t, pl.ds(r, LEVELS, stride=ROWS), :]
                else:
                    tile = jnp.where(level < flat[t, pl.ds(r, 1), :], 1.0, 0.0)
                cells[f, r, t] = tile
                tiles.append(tile)
            edges[0, f] = jnp.where(mine, pltpu.roll(tiles[0], 3 * r, 1), edges[0, f])
            edges[1, f] = jnp.where(mine, pltpu.roll(tiles[1], 3 * r + 3, 1), edges[1, f])
        return _

    lax.fori_loop(0, ROWS, arrange, 0, unroll=16)


def prepare_call(lon_size, *arguments):
    f32 = jnp.float32
    vmem = pl.BlockSpec(memory_space=pltpu.VMEM)
    anywhere = pl.BlockSpec(memory_space=pl.ANY)
    return pl.pallas_call(
        functools.partial(prepare, lon_size),
        out_shape=(
            jax.ShapeDtypeStruct((5, ROWS, 2, LEVELS, LANES), f32),
            jax.ShapeDtypeStruct((2, 5, LEVELS, LANES), f32),
            jax.ShapeDtypeStruct((4, ROWS, COLS), f32),
            jax.ShapeDtypeStruct((2, 2, LEVELS, LANES), f32),
            jax.ShapeDtypeStruct((2,), jnp.int32),
        ),
        in_specs=[anywhere] * 9,
        out_specs=(vmem,) * 4 + (pl.BlockSpec(memory_space=pltpu.SMEM),),
        scratch_shapes=[
            pltpu.VMEM((4, 2, LEVELS * ROWS, LANES), f32),
            pltpu.VMEM((ROWS, COLS), jnp.int32),
            pltpu.VMEM((2, ROWS, LANES), f32),
            pltpu.SMEM((COLS,), jnp.int32),
            pltpu.SemaphoreType.DMA((13,)),
        ],
        name="prepare",
    )(*arguments)


class Links:
    SHIFTS = [(a, b) for a in (1, -1, 2, -2, 0) for b in (0, 1, -1) if (a, b) != (0, 0)]
    NEAR = [n for n, (a, b) in enumerate(SHIFTS) if abs(a) < 2]
    FAR = [n for n, (a, b) in enumerate(SHIFTS) if abs(a) == 2]

    def __init__(self, lon_size, lat_size, turn=None):
        self.lon = lax.axis_index("lon")
        self.lat = lax.axis_index("lat")
        self.lon_size, self.lat_size, self.turn = lon_size, lat_size, turn
        self.top = self.lat == lat_size - 1
        self.below = self.lat == lat_size - 2
        self.barrier = pltpu.get_barrier_semaphore()

    def fold_peer(self, s):
        return wrapped(self.turn - self.lon + s - 2, self.lon_size)

    def lat_ok(self, a):
        return jnp.logical_and(self.lat + a >= 0, self.lat + a <= self.lat_size - 1)

    def when_lat(self, a, body):
        if a == 0:
            body()
        else:
            pl.when(self.lat_ok(a))(body)

    def peer(self, a, b):
        return {"lat": self.lat + a, "lon": wrapped(self.lon + b, self.lon_size)}

    def greet(self, to):
        pl.semaphore_signal(self.barrier, inc=1, device_id=to, device_id_type=MESH)

    def meet(self, shifts, top_slots=(), below_slots=()):
        count = jnp.int32(0)
        for a, b in shifts:
            self.when_lat(a, lambda a=a, b=b: self.greet(self.peer(a, b)))
            count = count + (1 if a == 0 else self.lat_ok(a).astype(jnp.int32))
        fold_count = jnp.int32(len(below_slots))
        for s in top_slots:
            fold_count = fold_count + (self.fold_peer(s) != self.lon).astype(jnp.int32)
        if self.turn is not None:

            @pl.when(self.top)
            def _():
                for s in top_slots:
                    q = self.fold_peer(s)

                    @pl.when(q != self.lon)
                    def _():
                        self.greet({"lat": self.lat, "lon": q})

                for s in below_slots:
                    self.greet({"lat": self.lat - 1, "lon": self.fold_peer(s)})

            @pl.when(self.below)
            def _():
                for s in below_slots:
                    self.greet({"lat": self.lat + 1, "lon": self.fold_peer(s)})

            count = count + jnp.where(self.top, fold_count, 0)
            count = count + jnp.where(self.below, len(below_slots), 0)
        return count

    def copy(self, src, dst, sems, to):
        return pltpu.make_async_remote_copy(
            src_ref=src,
            dst_ref=dst,
            send_sem=sems.at[0],
            recv_sem=sems.at[1],
            device_id=to,
            device_id_type=MESH,
        )

    def rim_copy(self, n, own, margins, centre, blocks, sems):
        a, b = self.SHIFTS[n]
        to = self.peer(a, b)
        if b:
            side = 1 if b == 1 else 0
            return self.copy(margins.at[side], blocks.at[2 - a, side], sems.at[:, n], to)
        src_rows, dst_rows = {
            1: ((0, 16), (8, 24)),
            2: ((8, 16), (0, 8)),
            -1: ((0, 16), (MARGIN + 16, MARGIN + 32)),
            -2: ((0, 8), (MARGIN + 32, MARGIN + 40)),
        }[a]
        return self.copy(
            own.at[:, src_rows[0] : src_rows[1]],
            centre.at[:, dst_rows[0] : dst_rows[1]],
            sems.at[:, n],
            to,
        )

    def far_copy(self, n, own, margins, rows, blocks, sems):
        a, b = self.SHIFTS[n]
        to = self.peer(a, b)
        side = 0 if a > 0 else 1
        if b:
            edge = 1 if b == 1 else 0
            return self.copy(margins.at[edge], blocks.at[side, edge], sems.at[:, n], to)
        src = slice(8, 16) if a > 0 else slice(0, 8)
        return self.copy(own.at[:, src], rows.at[side], sems.at[:, n], to)

    def fold_start(self, s, copy, src, dst, sem, same_lat):
        if not same_lat:
            copy().start()
            return
        own = self.fold_peer(s) == self.lon

        @pl.when(jnp.logical_not(own))
        def _():
            copy().start()

        @pl.when(own)
        def _():
            pltpu.make_async_copy(src, dst, sem).start()

    def fold_sent(self, s, copy, same_lat):
        if not same_lat:
            copy().wait_send()
            return

        @pl.when(self.fold_peer(s) != self.lon)
        def _():
            copy().wait_send()

    def fold_rim_ref(self, kind, s, src, dst):
        rows = (0, 16) if kind == 0 else (8, 16)
        to = {0: (0, 16), 1: (8, 16), 2: (16, 24)}[kind]
        lanes = slice(*{0: (128, 256), 3: (0, 128)}.get(s, (0, 256)))
        slot = s - (4 - dst.shape[0]) // 2
        return src.at[:, rows[0] : rows[1], lanes], dst.at[slot, :, to[0] : to[1], lanes]

    def fold_rim_copy(self, kind, s, src, dst, sems):
        a, b = self.fold_rim_ref(kind, s, src, dst)
        to = {"lat": self.lat + (0, -1, 1)[kind], "lon": self.fold_peer(s)}
        return self.copy(a, b, sems.at[:, 0 if kind == 0 else 1, s], to)

    def fold_rim_kinds(self, slots, kinds, body):
        @pl.when(self.top)
        def _():
            for s in slots:
                for kind in (0, 1):
                    if kind in kinds:
                        body(kind, s)

        @pl.when(self.below)
        def _():
            for s in slots:
                body(2, s)

    def fold_rim_start(self, slots, kinds, src, dst, sems):
        def body(kind, s):
            a, b = self.fold_rim_ref(kind, s, src, dst)
            self.fold_start(
                s,
                lambda: self.fold_rim_copy(kind, s, src, dst, sems),
                a,
                b,
                sems.at[1, 0, s],
                kind == 0,
            )

        self.fold_rim_kinds(slots, kinds, body)

    def fold_rim_finish(self, slots, kinds, src, dst, sems):
        @pl.when(self.top)
        def _():
            for s in slots:
                self.fold_rim_copy(0, s, src, dst, sems).wait_recv()
                self.fold_rim_copy(2, s, src, dst, sems).wait_recv()

        if 1 in kinds:

            @pl.when(self.below)
            def _():
                for s in slots:
                    self.fold_rim_copy(1, s, src, dst, sems).wait_recv()

        self.fold_rim_kinds(
            slots,
            kinds,
            lambda kind, s: self.fold_sent(
                s, lambda: self.fold_rim_copy(kind, s, src, dst, sems), kind == 0
            ),
        )


def first_exchange(
    lon_size, lat_size, turn, cells, edges, rim, margins, bands, edges_in, fold_cells, fold_rim, far_rows, far_blocks,
    far_sem, edge_sem, band_sem, wet_sem, fold_sem, fold_wet_sem, fold_rim_sem
):
    links = Links(lon_size, lat_size, turn)
    far = [Links.SHIFTS[n] for n in Links.FAR]
    count = links.meet([(1, 0), (-1, 0), (0, 1), (0, -1)] + far, (1, 2), (1, 2))
    pl.semaphore_wait(links.barrier, count)

    def edge_copy(side):
        return links.copy(
            edges.at[side], edges_in.at[side], edge_sem.at[:, side], links.peer(0, 2 * side - 1)
        )

    def band_copies(side):
        first = ROWS - 3 if side == 0 else 0
        wet_from, wet_to = (ROWS - 1, 2) if side == 0 else (0, 0)
        to = links.peer(1 - 2 * side, 0)
        return (
            links.copy(
                cells.at[0:4, first : first + 3], bands.at[side, 0:4], band_sem.at[:, side], to
            ),
            links.copy(cells.at[4, wet_from], bands.at[side, 4, wet_to], wet_sem.at[:, side], to),
        )

    fold_parts = (
        lambda s: (cells.at[0:4, ROWS - 3 : ROWS], fold_cells.at[s - 1, 0:4], fold_sem.at[:, s - 1]),
        lambda s: (cells.at[4, ROWS - 1], fold_cells.at[s - 1, 4, 2], fold_wet_sem.at[:, s - 1]),
    )

    def fold_cell_copy(s, part):
        return links.copy(*part(s), {"lat": links.lat, "lon": links.fold_peer(s)})

    for side in range(2):

        def send(side=side):
            for copy in band_copies(side):
                copy.start()

        links.when_lat(1 - 2 * side, send)
    for side in range(2):
        edge_copy(side).start()
    def far_copy(n):
        return links.far_copy(n, rim, margins, far_rows, far_blocks, far_sem)

    for n in Links.FAR:
        links.when_lat(Links.SHIFTS[n][0], lambda n=n: far_copy(n).start())

    @pl.when(links.top)
    def _():
        for s in (1, 2):
            for part in fold_parts:
                a, b, sem = part(s)
                links.fold_start(
                    s, lambda s=s, part=part: fold_cell_copy(s, part), a, b, sem.at[1], True
                )

    links.fold_rim_start((1, 2), (0, 2), rim, fold_rim, fold_rim_sem)

    for side in range(2):
        edge_copy(side).wait()
    for side in range(2):

        def arrived(side=side):
            for copy in band_copies(side):
                copy.wait_recv()

        def sent(side=side):
            for copy in band_copies(side):
                copy.wait_send()

        links.when_lat(2 * side - 1, arrived)
        links.when_lat(1 - 2 * side, sent)

    @pl.when(links.top)
    def _():
        for s in (1, 2):
            for part in fold_parts:
                fold_cell_copy(s, part).wait_recv()
                links.fold_sent(s, lambda s=s, part=part: fold_cell_copy(s, part), True)

    links.fold_rim_finish((1, 2), (0, 2), rim, fold_rim, fold_rim_sem)
    for n in Links.FAR:
        links.when_lat(-Links.SHIFTS[n][0], lambda n=n: far_copy(n).wait_recv())
    for n in Links.FAR:
        links.when_lat(Links.SHIFTS[n][0], lambda n=n: far_copy(n).wait_send())


def first_exchange_call(lon_size, lat_size, turn, collective_id):
    f32 = jnp.float32
    anywhere = pl.BlockSpec(memory_space=pl.ANY)
    dma = pltpu.SemaphoreType.DMA
    return pl.pallas_call(
        functools.partial(first_exchange, lon_size, lat_size, turn),
        out_shape=(
            jax.ShapeDtypeStruct((2, 5, 3, 2, LEVELS, LANES), f32),
            jax.ShapeDtypeStruct((2, 5, LEVELS, LANES), f32),
            jax.ShapeDtypeStruct((2, 5, 3, 2, LEVELS, LANES), f32),
            jax.ShapeDtypeStruct((2, 4, MARGIN, COLS), f32),
            jax.ShapeDtypeStruct((2, 4, 8, COLS), f32),
            jax.ShapeDtypeStruct((2, 2, 2, LEVELS, LANES), f32),
        ),
        in_specs=[anywhere] * 4,
        out_specs=(anywhere,) * 6,
        scratch_shapes=[dma((2, 14))] + [dma((2, 2))] * 5 + [dma((2, 2, 4))],
        compiler_params=pltpu.CompilerParams(
            collective_id=collective_id, has_side_effects=True, vmem_limit_bytes=4 << 20
        ),
        name="first_exchange",
    )


def interior(
    lon_size, lat_size, fold_ref, cells_in, edges, rim_in, bands, edges_in, fold_cells, fold_rim, rim_own, margins,
    centre, blocks, moved, done, means, mean_margins,
    cells, halo, face_west, flux_north, part, sums, ghost, ghost_margins, cell_sem, rim_sem, ghost_sem
):
    f32 = jnp.float32
    links = Links(lon_size, lat_size)
    lat = links.lat
    near = [(n, Links.SHIFTS[n]) for n in Links.NEAR]
    count = links.meet([shift for _, shift in near])
    filled = pltpu.make_async_copy(cells_in, cells.at[:, 3 : 3 + ROWS], cell_sem.at[0])
    south = pltpu.make_async_copy(bands.at[0], cells.at[:, 0:3], cell_sem.at[1])
    north = pltpu.make_async_copy(bands.at[1], cells.at[:, ROWS + 3 : ROWS + 6], cell_sem.at[2])
    keep = pltpu.make_async_copy(
        rim_own, centre.at[:, MARGIN : MARGIN + ROWS], cell_sem.at[3]
    )
    fold_in = pltpu.make_async_copy(ghost, centre.at[:, MARGIN + ROWS : WIDE], cell_sem.at[4])
    filled.start()
    keep.start()
    links.when_lat(-1, south.start)
    links.when_lat(1, north.start)

    @pl.when(lat == 0)
    def _():
        cells[:, 0:3] = jnp.zeros((5, 3, 2, LEVELS, LANES), f32)

    level = lax.broadcasted_iota(jnp.int32, (LEVELS, LANES), 0)
    lane = lax.broadcasted_iota(jnp.int32, (LEVELS, LANES), 1)

    @pl.when(links.top)
    def _():
        turn_lanes, flip_rows, same_tile = turner(fold_ref)

        def image(tile):
            turned = [turn_lanes(tile(2 - n), tile(3 - n)) for n in range(3)]
            return [jnp.where(same_tile, turned[t], turned[t + 1]) for t in range(2)]

        def across(g, _):
            for f in range(4):
                for t, value in enumerate(image(lambda n: fold_cells[n // 2, f, 2 - g, n % 2])):
                    cells[f, ROWS + 3 + g, t] = -value if f < 2 else value
            return _

        lax.fori_loop(0, 3, across, 0)
        for t, value in enumerate(image(lambda n: fold_cells[n // 2, 4, 2, n % 2])):
            cells[4, ROWS + 3, t] = value

        def across_rim(f, _):
            sign = jnp.where(jnp.logical_or(f == SEA, f == TALLY), 1.0, -1.0)
            for q, first in enumerate((8, 0, 16)):

                def tile(n):
                    lanes = slice((n % 2) * LANES, (n % 2 + 1) * LANES)
                    return fold_rim[n // 2, f, first : first + 8, lanes]

                for t, value in enumerate(image(tile)):
                    ghost[f, 8 * q : 8 * q + 8, t * LANES : (t + 1) * LANES] = flip_rows(value) * sign
            return _

        lax.fori_loop(0, 4, across_rim, 0)
        fold_in.start()
        for block in range(2):
            for pair in range(2):
                tiles = []
                for g in range(4):
                    first = 8 * (g % 2) if block == 0 else 16
                    rows = slice(first, first + 8)
                    f = 2 * pair + g // 2
                    tiles.append((ghost[f, rows, 0:LANES], ghost[f, rows, LANES:COLS]))
                packed = pack_margins(tiles)
                for side in range(2):
                    ghost_margins[block, side, pair] = packed[side]

    def ghost_copies(row):
        for side in range(2):
            to = links.peer(-row, 2 * side - 1)
            if row == 0:
                yield links.copy(
                    ghost_margins.at[:, side], blocks.at[3:5, side], ghost_sem.at[:, side], to
                )
            else:
                yield links.copy(
                    ghost_margins.at[0, side], blocks.at[4, side], ghost_sem.at[:, 2 + side], to
                )
        if row:
            yield links.copy(
                ghost.at[:, 0:8],
                centre.at[:, MARGIN + 32 : WIDE],
                ghost_sem.at[:, 4],
                links.peer(-1, 0),
            )

    def back(x, n):
        return pltpu.roll(x, LANES - n, 1)

    packed = []
    for f in range(5):
        west = edges_in[1, f]
        own = edges[0, f]
        packed.append((west, own))
    speed = 0.5 * (back(packed[0][0], 2) + packed[0][1]) * back(packed[4][0], 2) * packed[4][1]
    face_west[4] = speed
    for f in range(4):
        west, own = packed[f]
        inner = back(west, 2)
        ew = back(west, 1) - west
        eo = back(own, 1) - own
        face_west[f] = weno_flux(
            ew,
            back(ew, 1),
            own - inner,
            eo,
            back(eo, 1),
            inner,
            own,
            COURANT * speed,
            (COURANT / 6.0) * jnp.abs(speed),
            speed >= 0.0,
        )


    def unpack(r, _):
        for f in range(5):
            east = pltpu.roll(edges_in[0, f], LANES - 3 * r, 1)
            west = pltpu.roll(edges_in[1, f], LANES - 3 - 3 * r, 1)
            halo[f, r] = jnp.where(lane < LANES // 2, east, west)
        return _

    lax.fori_loop(0, ROWS, unpack, 0, unroll=16)

    def rim_copy(n):
        return links.rim_copy(n, rim_own, margins, centre, blocks, rim_sem)

    pl.semaphore_wait(links.barrier, count)
    for n, (a, b) in near:
        links.when_lat(a, lambda n=n: rim_copy(n).start())

    @pl.when(links.top)
    def _():
        for row in range(2):
            for copy in ghost_copies(row):
                copy.start()

    def north_face(face, cells, first):
        def at(f, row, t):
            return cells[f, row - first, t]

        speeds = []
        for t in range(2):
            speed = (
                0.5
                * (at(1, face - 1, t) + at(1, face, t))
                * at(4, face - 1, t)
                * at(4, face, t)
            )
            flux_north[4, face, t] = speed
            speeds.append(
                (COURANT * speed, (COURANT / 6.0) * jnp.abs(speed), speed >= 0.0)
            )
        for f in range(4):
            for t in range(2):
                q = [at(f, face + n - 3, t) for n in range(6)]
                e = [q[n + 1] - q[n] for n in range(5)]
                flux_north[f, face, t] = weno_flux(*e, q[2], q[3], *speeds[t])

    def north_loop(face, _):
        north_face(face, cells_in, 0)
        return _

    lax.fori_loop(3, 14, north_loop, 0, unroll=11)

    def ahead(x, n, count=2):
        return [
            pltpu.roll(jnp.where(lane < n, x[(t + 1) % 3], x[t]), LANES - n, 1)
            for t in range(count)
        ]

    def behind(x, n):
        return [
            pltpu.roll(jnp.where(lane >= LANES - n, x[(t + 2) % 3], x[t]), n, 1) for t in range(2)
        ]

    def east_loop(r, _):
        wet = [cells_in[4, r, 0], cells_in[4, r, 1], halo[4, r]]
        wet_next = ahead(wet, 1)
        gaps, nexts, firsts = [], [], []
        for f in range(4):
            q = [cells_in[f, r, 0], cells_in[f, r, 1], halo[f, r]]
            nxt = ahead(q, 1, 3)
            firsts.append(q)
            nexts.append(nxt)
            gaps.append([nxt[n] - q[n] for n in range(3)])
        speeds = []
        for t in range(2):
            speed = 0.5 * (firsts[0][t] + nexts[0][t]) * wet[t] * wet_next[t]
            speeds.append(speed)
        trails = []

        def difference(x, first):
            west = behind([x[0], x[1], first], 1)
            return x[0] - west[0], x[1] - west[1]

        def west_of(f):
            return pltpu.roll(face_west[f], LANES - 1 - 3 * r, 1)

        spread = difference(speeds, west_of(4))
        for t in range(2):
            part[4, r, t] = spread[t]
        for f in range(4):
            e = gaps[f]
            em1 = behind(e, 1)
            em2 = behind(e, 2)
            ep1 = ahead(e, 1)
            ep2 = ahead(e, 2)
            trails.append(em1)
            flux = [
                weno_flux(
                    em2[t],
                    em1[t],
                    e[t],
                    ep1[t],
                    ep2[t],
                    firsts[f][t],
                    nexts[f][t],
                    COURANT * speeds[t],
                    (COURANT / 6.0) * jnp.abs(speeds[t]),
                    speeds[t] >= 0.0,
                )
                for t in range(2)
            ]
            lost = difference(flux, west_of(f))
            for t in range(2):
                part[f, r, t] = lost[t]
        for t in range(2):
            part[5, r, t] = 0.8 * (gaps[3][t] + trails[3][t]) - 0.2 * (
                gaps[2][t] + trails[2][t]
            )
        return _

    lax.fori_loop(0, ROWS, east_loop, 0, unroll=4)

    filled.wait()
    links.when_lat(-1, south.wait)
    links.when_lat(1, north.wait)

    def outer_loop(n, _):
        north_face(n, cells, -3)
        north_face(n + 14, cells, -3)
        return _

    lax.fori_loop(0, 3, outer_loop, 0)

    def down_sum(x):
        for s in (1, 2, 4):
            x = x + jnp.where(level >= s, pltpu.roll(x, s, 0), 0.0)
        return x

    def up_sum(x):
        for s in (1, 2, 4):
            x = x + jnp.where(level < LEVELS - s, pltpu.roll(x, LEVELS - s, 0), 0.0)
        return x

    total_rows = ROWS * lat_size

    def combine(r, _):
        row = (lat * ROWS + r).astype(f32)
        coriolis = CORIOLIS * (2.0 * (row + 0.5) / total_rows - 1.0)
        for t in range(2):
            q = [cells[f, r + 3, t] for f in range(4)]
            wet = cells[4, r + 3, t]
            spread = part[4, r, t] + (flux_north[4, r + 1, t] - flux_north[4, r, t])
            lift = jnp.where(level >= 1, (-0.5 * COURANT) * up_sum(spread), 0.0)
            rates = []
            for f in range(4):
                vertical = lift * (pltpu.roll(q[f], 1, 0) + q[f])
                rates.append(
                    (pltpu.roll(vertical, LEVELS - 1, 0) - vertical)
                    - part[f, r, t]
                    - (flux_north[f, r + 1, t] - flux_north[f, r, t])
                )
            slope_east = part[5, r, t]
            slope_north = 0.8 * (cells[3, r + 4, t] - cells[3, r + 2, t]) - 0.2 * (
                cells[2, r + 4, t] - cells[2, r + 2, t]
            )
            grad_east = 0.5 * (down_sum(slope_east) - 0.5 * slope_east)
            grad_north = 0.5 * (down_sum(slope_north) - 0.5 * slope_north)
            force_zonal = rates[0] + coriolis * q[1] - PRESSURE_GAIN * grad_east
            force_merid = rates[1] - coriolis * q[0] - PRESSURE_GAIN * grad_north
            sums[0, t, pl.ds(r, 1), :] = jnp.sum(wet * force_zonal, axis=0, keepdims=True)
            sums[1, t, pl.ds(r, 1), :] = jnp.sum(wet * force_merid, axis=0, keepdims=True)
            moved[0, r, t] = q[0] + force_zonal
            moved[1, r, t] = q[1] + force_merid
            done[0, t, pl.ds(r, LEVELS, stride=ROWS), :] = wet * (q[2] + rates[2])
            done[1, t, pl.ds(r, LEVELS, stride=ROWS), :] = wet * (q[3] + rates[3])
        return _

    lax.fori_loop(0, ROWS, combine, 0, unroll=4)

    for t in range(2):
        lanes = slice(t * LANES, (t + 1) * LANES)
        column = jnp.maximum(rim_in[TALLY, :, lanes], 1.0)
        for f in range(2):
            sums[f, t] = sums[f, t] / column
            means[f, :, lanes] = sums[f, t]
    tiles = []
    for g in range(4):
        rows = slice(8 * (g % 2), 8 * (g % 2) + 8)
        tiles.append((sums[g // 2, 0, rows, :], sums[g // 2, 1, rows, :]))
    mean_margins[0, 0], mean_margins[1, 0] = pack_margins(tiles)

    keep.wait()
    for n, (a, b) in near:
        links.when_lat(-a, lambda n=n: rim_copy(n).wait_recv())
    for n, (a, b) in near:
        links.when_lat(a, lambda n=n: rim_copy(n).wait_send())

    @pl.when(links.top)
    def _():
        fold_in.wait()
        for copy in ghost_copies(0):
            copy.wait_recv()
        for row in range(2):
            for copy in ghost_copies(row):
                copy.wait_send()

    @pl.when(links.below)
    def _():
        for copy in ghost_copies(1):
            copy.wait_recv()


def interior_call(lon_size, lat_size, collective_id):
    f32 = jnp.float32
    vmem = pl.BlockSpec(memory_space=pltpu.VMEM)
    anywhere = pl.BlockSpec(memory_space=pl.ANY)
    dma = pltpu.SemaphoreType.DMA
    return pl.pallas_call(
        functools.partial(interior, lon_size, lat_size),
        out_shape=(
            jax.ShapeDtypeStruct((4, WIDE, COLS), f32),
            jax.ShapeDtypeStruct((5, 2, 2, LEVELS, LANES), f32),
            jax.ShapeDtypeStruct((2, ROWS, 2, LEVELS, LANES), f32),
            jax.ShapeDtypeStruct((2, 2, LEVELS * ROWS, LANES), f32),
            jax.ShapeDtypeStruct((2, ROWS, COLS), f32),
            jax.ShapeDtypeStruct((2, 1, LEVELS, LANES), f32),
        ),
        in_specs=[pl.BlockSpec(memory_space=pltpu.SMEM)]
        + [vmem, vmem, vmem, anywhere, vmem, vmem, vmem, anywhere, anywhere],
        out_specs=(anywhere, anywhere, vmem, vmem, vmem, vmem),
        scratch_shapes=[
            pltpu.VMEM((5, ROWS + 6, 2, LEVELS, LANES), f32),
            pltpu.VMEM((5, ROWS, LEVELS, LANES), f32),
            pltpu.VMEM((5, LEVELS, LANES), f32),
            pltpu.VMEM((5, ROWS + 1, 2, LEVELS, LANES), f32),
            pltpu.VMEM((6, ROWS, 2, LEVELS, LANES), f32),
            pltpu.VMEM((2, 2, ROWS, LANES), f32),
            pltpu.VMEM((4, MARGIN, COLS), f32),
            pltpu.VMEM((2, 2, 2, LEVELS, LANES), f32),
            dma((5,)),
            dma((2, 14)),
            dma((2, 5)),
        ],
        compiler_params=pltpu.CompilerParams(
            collective_id=collective_id, has_side_effects=True, vmem_limit_bytes=12 << 20
        ),
        name="interior",
    )


def second_exchange(
    lon_size, lat_size, turn, means, margins, centre, blocks, fold_rim, rim_sem, fold_rim_sem
):
    links = Links(lon_size, lat_size, turn)
    count = links.meet(Links.SHIFTS, (0, 1, 2, 3), (0, 1, 2, 3))
    pl.semaphore_wait(links.barrier, count)
    slots, kinds = (0, 1, 2, 3), (0, 1, 2)

    def rim_copy(n):
        return links.rim_copy(n, means, margins, centre, blocks, rim_sem)

    links.fold_rim_start(slots, kinds, means, fold_rim, fold_rim_sem)
    for n, (a, b) in enumerate(Links.SHIFTS):
        links.when_lat(a, lambda n=n: rim_copy(n).start())
    for n, (a, b) in enumerate(Links.SHIFTS):
        links.when_lat(-a, lambda n=n: rim_copy(n).wait_recv())
    links.fold_rim_finish(slots, kinds, means, fold_rim, fold_rim_sem)
    for n, (a, b) in enumerate(Links.SHIFTS):
        links.when_lat(a, lambda n=n: rim_copy(n).wait_send())


def second_exchange_call(lon_size, lat_size, turn, collective_id):
    f32 = jnp.float32
    anywhere = pl.BlockSpec(memory_space=pl.ANY)
    dma = pltpu.SemaphoreType.DMA
    return pl.pallas_call(
        functools.partial(second_exchange, lon_size, lat_size, turn),
        out_shape=(
            jax.ShapeDtypeStruct((2, WIDE, COLS), f32),
            jax.ShapeDtypeStruct((5, 2, 1, LEVELS, LANES), f32),
            jax.ShapeDtypeStruct((4, 2, MARGIN, COLS), f32),
        ),
        in_specs=[anywhere] * 2,
        out_specs=(anywhere,) * 3,
        scratch_shapes=[dma((2, 14)), dma((2, 2, 4))],
        compiler_params=pltpu.CompilerParams(
            collective_id=collective_id, has_side_effects=True, vmem_limit_bytes=4 << 20
        ),
        name="second_exchange",
    )


def finish(
    lat_size, fold_ref, far_rows, far_blocks, centre_a, blocks_a, centre_b, blocks_b, fold_b, means, rim_own, moved, done_in,
    u_out, v_out, t_out, s_out, sea_out, zon_out, mer_out,
    wave, done, flat, tally, sems
):
    f32 = jnp.float32
    lat = lax.axis_index("lat")
    total_rows = ROWS * lat_size
    width = COLS + LANES
    stores = []
    for f, ref in ((2, t_out), (3, s_out)):
        for t in range(2):
            lanes = slice(t * LANES, (t + 1) * LANES)
            stores.append(pltpu.make_async_copy(done_in.at[f - 2, t], ref.at[:, lanes], sems.at[2 * f + t]))
    for copy in stores:
        copy.start()

    lane = lax.broadcasted_iota(jnp.int32, (LEVELS, LANES), 1)
    own_rows = slice(MARGIN, MARGIN + ROWS)
    row = lax.broadcasted_iota(jnp.int32, (WIDE, width), 0) + (lat * ROWS - MARGIN)

    def side_tile(from_east, from_west, n, part):
        lead = MARGIN * (2 * (n % 2) + part)
        if lead:
            from_east = pltpu.roll(from_east, LANES - lead, 1)
        from_west = pltpu.roll(from_west, LANES - MARGIN - lead, 1)
        return jnp.where(lane < LANES // 2, from_east, from_west)

    sources = ((0, 1), (1, 0), (1, 1), (2, 0), (2, 1), (3, 0), (3, 1), (4, 0))
    for f in range(6):
        centre, blocks, n = (centre_a, blocks_a, f) if f < 4 else (centre_b, blocks_b, f - 4)
        wave[f, :, 0:COLS] = centre[n]
        for i in range(8):
            block, part = sources[i]
            wave[f, 8 * i : 8 * i + 8, COLS:width] = side_tile(
                blocks[block, 0, n // 2], blocks[block, 1, n // 2], n, part
            )
    for side, rows, part, here in ((0, 0, 1, lat > 1), (1, WIDE - 8, 0, lat < lat_size - 2)):

        @pl.when(here)
        def _():
            for f in range(4):
                wave[f, rows : rows + 8, 0:COLS] = far_rows[side, f]
                wave[f, rows : rows + 8, COLS:width] = side_tile(
                    far_blocks[side, 0, f // 2], far_blocks[side, 1, f // 2], f, part
                )

    for f in range(2):
        wave[MEANZ + f, own_rows, 0:COLS] = means[f]
    for n, empty in ((0, MARGIN), (1, 8)):

        @pl.when(lat == n)
        def _():
            wave[0:6, 0:empty] = jnp.zeros((6, empty, width), f32)

    def unfold(ghost_tiles):
        turn_lanes, flip_rows, same_tile = turner(fold_ref)

        def mean(n, _):
            for to, source in ghost_tiles:

                def tile(m):
                    at = slice((m % 2) * LANES, (m % 2 + 1) * LANES)
                    return fold_b[m // 2, n, source : source + 8, at]

                turned = {m: turn_lanes(tile(m + 4), tile(m + 5)) for m in range(-3, 2)}
                image = {
                    m: -flip_rows(jnp.where(same_tile, turned[m], turned[m - 1]))
                    for m in range(-2, 2)
                }
                f = n + MEANZ
                wave[f, to : to + 8, 0:128] = image[0]
                wave[f, to : to + 8, 128:256] = image[-1]
                wave[f, to : to + 8, 256:384] = jnp.where(lane < LANES // 2, image[-2], image[1])
            return _

        lax.fori_loop(0, 2, mean, 0)

    pl.when(lat == lat_size - 1)(lambda: unfold(((40, 8), (48, 0), (56, 16))))
    pl.when(lat == lat_size - 2)(lambda: unfold(((56, 8),)))

    mirrored = jnp.minimum(row, 2 * total_rows - 1 - row).astype(f32)
    wide_tally = wave[TALLY]
    wave[6] = jnp.where(wide_tally > 0.0, 1.0, 0.0)
    wave[TALLY] = wide_tally * (0.5 * WAVE_MASS / LEVELS)
    wave[7] = (CORIOLIS / SUBSTEPS) * (2.0 * (mirrored + 0.5) / total_rows - 1.0)
    wave[MEANZ] = wave[MEANZ] * (1.0 / SUBSTEPS)
    wave[MEANM] = wave[MEANM] * (1.0 / SUBSTEPS)

    def east_difference(x):
        return pltpu.roll(x, width - 1, 1) - pltpu.roll(x, 1, 1)

    def north_difference(x):
        return pltpu.roll(x, x.shape[0] - 1, 0) - pltpu.roll(x, 1, 0)

    def substep(rows):
        thick = wave[TALLY, rows]
        wet = wave[6, rows]
        zonal = wave[ZON, rows]
        merid = wave[MER, rows]
        level_next = wet * (
            wave[SEA, rows] - (east_difference(thick * zonal) + north_difference(thick * merid))
        )
        turn_rate = wave[7, rows]
        wave[SEA, rows] = level_next
        wave[ZON, rows] = wet * (
            zonal
            - (0.5 * WAVE_MOMENTUM) * east_difference(level_next)
            + (turn_rate * merid + wave[MEANZ, rows])
        )
        wave[MER, rows] = wet * (
            merid
            - (0.5 * WAVE_MOMENTUM) * north_difference(level_next)
            + (wave[MEANM, rows] - turn_rate * zonal)
        )

    for stage in range(SUBSTEPS // 4):
        rows = slice(8 * stage, WIDE - 8 * stage)
        lax.fori_loop(0, 4, lambda n, _: (substep(rows), _)[1], 0, unroll=2)

    for f, ref in enumerate((sea_out, zon_out, mer_out)):
        copy = pltpu.make_async_copy(wave.at[f, own_rows, 0:COLS], ref, sems.at[8 + f])
        copy.start()
        stores.append(copy)
    for t in range(2):
        lanes = slice(t * LANES, (t + 1) * LANES)
        tally[t] = rim_own[TALLY, :, lanes]
        for f in range(2):
            flat[f, t] = wave[ZON + f, own_rows, lanes] - rim_own[ZON + f, :, lanes] - means[f, :, lanes]
    level = lax.broadcasted_iota(jnp.int32, (LEVELS, LANES), 0).astype(f32)

    def last(r, _):
        for t in range(2):
            wet = level < tally[t, pl.ds(r, 1), :]
            for f in range(2):
                shift = flat[f, t, pl.ds(r, 1), :]
                done[f, t, pl.ds(r, LEVELS, stride=ROWS), :] = jnp.where(
                    wet, moved[f, r, t] + shift, 0.0
                )
        return _

    lax.fori_loop(0, ROWS, last, 0, unroll=16)

    for f, ref in ((0, u_out), (1, v_out)):
        for t in range(2):
            lanes = slice(t * LANES, (t + 1) * LANES)
            copy = pltpu.make_async_copy(done.at[f, t], ref.at[:, lanes], sems.at[2 * f + t])
            copy.start()
            stores.append(copy)
    for copy in stores:
        copy.wait()


def finish_call(lat_size, *arguments):
    f32 = jnp.float32
    deep = jax.ShapeDtypeStruct((LEVELS * ROWS, COLS), f32)
    flat = jax.ShapeDtypeStruct((ROWS, COLS), f32)
    vmem = pl.BlockSpec(memory_space=pltpu.VMEM)
    anywhere = pl.BlockSpec(memory_space=pl.ANY)
    return pl.pallas_call(
        functools.partial(finish, lat_size),
        out_shape=(deep,) * 4 + (flat,) * 3,
        in_specs=[pl.BlockSpec(memory_space=pltpu.SMEM)] + [vmem] * 11,
        out_specs=(anywhere,) * 7,
        scratch_shapes=[
            pltpu.VMEM((8, WIDE, COLS + LANES), f32),
            pltpu.VMEM((2, 2, LEVELS * ROWS, LANES), f32),
            pltpu.VMEM((2, 2, ROWS, LANES), f32),
            pltpu.VMEM((2, ROWS, LANES), f32),
            pltpu.SemaphoreType.DMA((11,)),
        ],
        compiler_params=pltpu.CompilerParams(vmem_limit_bytes=12 << 20),
        name="finish",
    )(*arguments)


def on_device(lon_size, lat_size, *arguments):
    *fields, sea, zon, mer, tally, seam = arguments
    deep = [x.reshape(LEVELS * ROWS, COLS) for x in fields]
    cells, edges, rim_own, margins, fold = prepare_call(lon_size, *deep, sea, zon, mer, tally, seam)
    turn = fold[0]
    bands, edges_in, fold_cells, fold_a, far_rows, far_blocks = lax.switch(
        turn,
        [first_exchange_call(lon_size, lat_size, n, n) for n in range(lon_size)],
        cells,
        edges,
        rim_own,
        margins,
    )
    centre_a, blocks_a, moved, done, means, mean_margins = interior_call(
        lon_size, lat_size, 2 * lon_size
    )(fold, cells, edges, rim_own, bands, edges_in, fold_cells, fold_a, rim_own, margins)
    centre_b, blocks_b, fold_b = lax.switch(
        turn,
        [second_exchange_call(lon_size, lat_size, n, lon_size + n) for n in range(lon_size)],
        means,
        mean_margins,
    )
    out = finish_call(
        lat_size, fold, far_rows, far_blocks, centre_a, blocks_a, centre_b, blocks_b, fold_b, means, rim_own,
        moved, done
    )
    return tuple(x.reshape(LEVELS, ROWS, COLS) for x in out[:4]) + tuple(out[4:])


def solution(mesh):
    deep = P(None, "lat", "lon")
    flat = P("lat", "lon")
    return jax.shard_map(
        functools.partial(on_device, mesh.shape["lon"], mesh.shape["lat"]),
        mesh=mesh,
        in_specs=(deep,) * 4 + (flat,) * 4 + (P("lon"),),
        out_specs=(deep,) * 4 + (flat,) * 3,
        check_vma=False,
    )
```
